32 devices in a mesh: snap: 2 (over y), chan: 16 (over z, x, core).
Axes of the slice: x: 2, y: 2, z: 4, core: 2. Of those that a mesh axis runs over, the one named last changes fastest.
Arguments:
- snap_tiles: bfloat16 [16, 192, 64, 128], P('snap', 'chan'), may hold values from -6 to 6
- beam_gain: float32 [16, 64, 128], P('snap'), may hold values from 0.1 to 1
- kernel: bfloat16 [16, 32, 128, 256], P(None, 'snap'), may hold values from -0.5 to 0.5
- tile_map: int32 [16, 32], replicated, may hold values from 0 to 63
- pixel_lm: float32 [2, 8192], P(None, 'snap'), may hold values from -0.5 to 0.5
- mode_uv: int32 [2, 2048], replicated, may hold values from -32 to 31
Outputs:
- sky_cube: float32 [32, 192, 256], P('snap', 'chan')
- delay_spec: float32 [2, 192, 2048], P(None, None, ('snap', 'chan'))
The draws below stay inside these ranges and needn't reach their ends.
Inputs may be any that keep to these rules, and one draw needn't show every extreme that they name: `tile_map`: tile indices.
All inputs are finite; a program needn't handle non-finite values.
Results may differ from the reference program's by a relative error of at most 0.0047.
Values may be sent and summed in bfloat16 or wider, within the bound.
No kernel may reach another device: no remote copies, remote signals or barrier semaphores. Data moves between devices by JAX's collectives and lax.ppermute only.
A program may use at most 192 MiB of HBM per device.

```python
import math
import jax
import jax.numpy as jnp
from jax import lax

SNAPS = 16
CHANS = 192
TILES = 64
TILE_PIX = 128
BLOCK_PIX = 256
PIXELS = 8192
BLOCKS = 32
MODES = 2048
UV_MAX = 32


def place_ends(array, rng, least, top_value):
    place = [jax.random.randint(jax.random.fold_in(rng, axis), (), 0, length) for axis, length in enumerate(array.shape)]
    longest = array.shape.index(max(array.shape))
    next_to = place[:longest] + [(place[longest] + 1) % array.shape[longest]] + place[longest + 1:]
    return array.at[tuple(place)].set(least).at[tuple(next_to)].set(top_value)


def block_levels(own_key, shape, pieces, smallest, top_value):
    gain = 1.0
    for dim, parts in pieces:
        heights = jax.random.uniform(jax.random.fold_in(jax.random.fold_in(own_key, 6), dim), (parts,), jnp.float32, smallest / len(pieces), top_value / len(pieces))
        gain = gain * jnp.repeat(jnp.exp(heights), shape[dim] // parts).reshape((-1,) + (1,) * (len(shape) - 1 - dim))
    return gain


def scatter_about(own_key, shape, scale, most, cuts=(), kind=jnp.bfloat16):
    array = jax.random.normal(own_key, shape, jnp.float32) * scale
    if len(cuts) > 0:
        array = block_levels(own_key, shape, cuts, -0.22, 0.18) * array
    return jnp.clip(array, min=-most, max=most).astype(kind)


def setup_inputs(seed: int = 0) -> dict:
    key_of = jax.random.split(jax.random.key(seed), 7)
    return {
        "snap_tiles": scatter_about(key_of[0], (SNAPS, CHANS, TILES, TILE_PIX), 1.0, 6.0, ((0, 2), (1, 16))),
        "beam_gain": jnp.clip(jnp.exp(math.log(1.0) - 2.3025851 * jax.random.uniform(key_of[1], (SNAPS, TILES, TILE_PIX), jnp.float32) ** block_levels(key_of[1], (SNAPS, TILES, TILE_PIX), ((0, 2),), -0.2, 0.2)), 0.1, 1.0),
        "kernel": scatter_about(key_of[2], (SNAPS, BLOCKS, TILE_PIX, BLOCK_PIX), TILE_PIX ** -0.5, 0.5, ((1, 2),)),
        "tile_map": place_ends(jax.random.randint(key_of[3], (SNAPS, BLOCKS), 0, TILES), jax.random.fold_in(key_of[3], 1), 0, TILES - 1).astype(jnp.int32),
        "pixel_lm": jnp.clip(jax.random.uniform(key_of[4], (2, PIXELS), jnp.float32, -0.5, 0.5) * block_levels(key_of[4], (2, PIXELS), ((1, 2),), -0.4, 0.0), -0.5, 0.5),
        "mode_uv": place_ends(jax.random.randint(key_of[5], (2, MODES), 0 - UV_MAX, UV_MAX), jax.random.fold_in(key_of[5], 1), 0 - UV_MAX, UV_MAX - 1).astype(jnp.int32),
    }


def hamming(length):
    channel_index = jnp.arange(length, dtype=jnp.float32)
    return 0.54 - 0.46 * jnp.cos(channel_index * (2.0 * math.pi / (length - 1)))

def delay_transform(power_spectrum):
    length = power_spectrum.shape[1]
    channel_index = jnp.arange(length, dtype=jnp.int32)
    residues = channel_index[:, None] * channel_index[None, :] % length
    phases = residues.astype(jnp.float32) * (2.0 * math.pi / length)
    cosine = jnp.cos(phases)
    sine_part = jnp.sin(phases)
    window_gain = hamming(length)[:, None]
    real_component = power_spectrum[0] * window_gain
    imag_part = power_spectrum[1] * window_gain
    highest = lax.Precision.HIGHEST
    out_re = jnp.dot(cosine, real_component, precision=highest) + jnp.dot(sine_part, imag_part, precision=highest)
    out_im = jnp.dot(cosine, imag_part, precision=highest) - jnp.dot(sine_part, real_component, precision=highest)
    return jnp.stack([out_re, out_im]) / math.sqrt(length)

def phasor(positions, uv_grid):
    spatial = uv_grid.astype(jnp.float32)
    phase_table = (positions[0][:, None] * spatial[0][None, :] + positions[1][:, None] * spatial[1][None, :]) * (2.0 * math.pi)
    return jnp.concatenate([jnp.cos(phase_table), -jnp.sin(phase_table)], axis=1).astype(jnp.bfloat16)

def reference(snap_tiles, beam_gain, kernel, tile_map, pixel_lm, mode_uv):
    weighted = (snap_tiles.astype(jnp.float32) * beam_gain[:, None]).astype(jnp.bfloat16)

    def add_snapshot(running, inputs):
        single_snapshot_tiles, one_kernel, one_map = inputs
        gathered_rows = jnp.take(single_snapshot_tiles, one_map.astype(jnp.int32), axis=1)
        block_term = jnp.einsum('cbt,btp->bcp', gathered_rows.astype(jnp.float32), one_kernel.astype(jnp.float32))
        return (running + block_term, None)
    zero_cube = jnp.zeros((BLOCKS, CHANS, BLOCK_PIX), jnp.float32)
    sky_cube, _ = lax.scan(add_snapshot, zero_cube, (weighted, kernel, tile_map))
    cube_low = sky_cube.astype(jnp.bfloat16)
    lm_blocks = pixel_lm.reshape(2, BLOCKS, BLOCK_PIX).transpose(1, 0, 2)

    def add_block(running, inputs):
        block_cube, block_lm = inputs
        phasor_lookup = phasor(block_lm, mode_uv)
        return (running + jnp.dot(block_cube, phasor_lookup, preferred_element_type=jnp.float32), None)
    zero_modes = jnp.zeros((CHANS, 2 * MODES), jnp.float32)
    summed, _ = lax.scan(add_block, zero_modes, (cube_low, lm_blocks))
    uv_modes = (summed / math.sqrt(PIXELS)).reshape(CHANS, 2, MODES).transpose(1, 0, 2)
    delay_spec = delay_transform(uv_modes)
    return (sky_cube, delay_spec)
```

```python
import math

import jax
import jax.numpy as jnp
import numpy as np
from jax import lax
from jax.experimental import pallas as pl
from jax.experimental.pallas import tpu as pltpu
from jax.sharding import PartitionSpec as P

BLOCK_PIX = 256
LANES = 128
UV_MAX = 32
TABLE_ROWS = 72


def delay_matrix(length):
    index = np.arange(length)
    window = 0.54 - 0.46 * np.cos(index * (2.0 * math.pi / (length - 1)))
    phase = (index[:, None] * index[None, :] % length) * (2.0 * math.pi / length)
    scale = window[:, None] / math.sqrt(length)
    cosine, sine = np.cos(phase) * scale, np.sin(phase) * scale
    return np.stack([np.stack([cosine, -sine], 1), np.stack([sine, cosine], 1)])


def turns(angle):
    r = (angle - jnp.round(angle)) * (2.0 * math.pi)
    return jnp.cos(r), jnp.sin(r)


def table(coord, rows):
    row = lax.broadcasted_iota(jnp.int32, (rows, coord.shape[1]), 0)
    k = jnp.where(row < UV_MAX, row, jnp.where(row < 2 * UV_MAX, row - (UV_MAX - 1), UV_MAX))
    cosine, sine = turns(k.astype(jnp.float32) * coord)
    is_sine = (row >= UV_MAX) & (row < 2 * UV_MAX)
    return jnp.where(row > 2 * UV_MAX, 0.0, jnp.where(is_sine, sine, cosine))


def gather_tiles(me, tile_map, snap_tiles, beam_gain, shifts, snap_count):
    local_snaps, chans, tiles, pix = snap_tiles.shape
    blocks = tile_map.shape[1] // snap_count
    first, count = shifts

    def body(me_ref, map_ref, tiles_ref, beam_ref, out_ref, scratch):
        s = pl.program_id(1)
        own = me_ref[0]
        dest = lax.rem(own + pl.program_id(0) + first, snap_count)
        value = tiles_ref[0].astype(jnp.float32) * beam_ref[...]
        scratch[...] = value.reshape(chans * tiles, pix)
        for b in range(blocks):
            t = map_ref[own * local_snaps + s, dest * blocks + b]
            rows = scratch[pl.ds(t, chans, stride=tiles), :]
            out_ref[0, b] = rows.astype(jnp.bfloat16)

    return pl.pallas_call(
        body,
        out_shape=jax.ShapeDtypeStruct((count, blocks, chans, local_snaps * pix), jnp.bfloat16),
        grid_spec=pltpu.PrefetchScalarGridSpec(
            num_scalar_prefetch=2,
            grid=(count, local_snaps),
            in_specs=[
                pl.BlockSpec((1, chans, tiles, pix), lambda j, s, *_: (s, 0, 0, 0)),
                pl.BlockSpec((1, tiles, pix), lambda j, s, *_: (s, 0, 0)),
            ],
            out_specs=pl.BlockSpec((1, blocks, chans, pix), lambda j, s, *_: (j, 0, 0, s)),
            scratch_shapes=[pltpu.VMEM((chans * tiles, pix), jnp.float32)],
        ),
        name="gather_tiles",
    )(me, tile_map, snap_tiles, beam_gain)


def own_part(me, own_tiles, kernel, pixel_lm):
    blocks, chans, depth = own_tiles.shape
    _, _, pix, width = kernel.shape
    local_snaps = depth // pix

    def body(me_ref, tiles_ref, kernel_ref, lm_ref, cube_ref, l_ref, m_ref):
        weights = kernel_ref[...].reshape(depth, width)
        cube_ref[0] = jnp.dot(tiles_ref[0], weights, preferred_element_type=jnp.float32)
        l_ref[...] = table(lm_ref[0:1, :], TABLE_ROWS)
        m_ref[...] = table(lm_ref[1:2, :], LANES).astype(jnp.bfloat16)

    pixels = blocks * width
    return pl.pallas_call(
        body,
        out_shape=(
            jax.ShapeDtypeStruct((blocks, chans, width), jnp.float32),
            jax.ShapeDtypeStruct((TABLE_ROWS, pixels), jnp.float32),
            jax.ShapeDtypeStruct((LANES, pixels), jnp.bfloat16),
        ),
        grid_spec=pltpu.PrefetchScalarGridSpec(
            num_scalar_prefetch=1,
            grid=(blocks,),
            in_specs=[
                pl.BlockSpec((1, chans, depth), lambda b, me: (b, 0, 0)),
                pl.BlockSpec((local_snaps, 1, pix, width), lambda b, me: (me[0], b, 0, 0)),
                pl.BlockSpec((2, width), lambda b, me: (0, b)),
            ],
            out_specs=(
                pl.BlockSpec((1, chans, width), lambda b, me: (b, 0, 0)),
                pl.BlockSpec((TABLE_ROWS, width), lambda b, me: (0, b)),
                pl.BlockSpec((LANES, width), lambda b, me: (0, b)),
            ),
        ),
        name="own_part",
    )(me, own_tiles, kernel, pixel_lm)


def uv_part(me, other_tiles, kernel, partial, l_table, m_table, mode_uv, snap_count, cells, scale):
    sources, blocks, chans, depth = other_tiles.shape
    _, _, pix, width = kernel.shape
    local_snaps = depth // pix
    modes = mode_uv.shape[1]
    owners = modes // cells
    sine_rows = slice(UV_MAX, 2 * UV_MAX)

    def select(acc, uv_ref, out_ref):
        for start in range(0, modes, LANES):
            u, v = uv_ref[0:1, start : start + LANES], uv_ref[1:2, start : start + LANES]
            sign_u = jnp.where(u < 0, -scale, scale).astype(jnp.float32)
            sign_v = jnp.where(v < 0, -1.0, 1.0).astype(jnp.float32)
            u, v = jnp.abs(u), jnp.abs(v)
            cos_lane = jnp.where(v == UV_MAX, 2 * UV_MAX, v)
            sin_lane = jnp.where(v == 0, LANES - 1, v + (UV_MAX - 1))
            cos_row = jnp.where(u == UV_MAX, 2 * UV_MAX, u)
            sin_row = jnp.where(u == 0, TABLE_ROWS - 1, u + (UV_MAX - 1))
            row = lax.broadcasted_iota(jnp.int32, (TABLE_ROWS, LANES), 0)
            is_cos = row == cos_row
            is_sin = row == sin_row
            in_sine = (row >= UV_MAX) & (row < 2 * UV_MAX)
            re_weight = jnp.where(in_sine, jnp.where(is_sin, -sign_u * sign_v, 0.0), jnp.where(is_cos, scale, 0.0))
            im_weight = jnp.where(in_sine, jnp.where(is_sin, -sign_u, 0.0), jnp.where(is_cos, -sign_v * scale, 0.0))
            cos_index = jnp.broadcast_to(cos_lane, (TABLE_ROWS, LANES))
            sin_index = jnp.broadcast_to(sin_lane, (TABLE_ROWS, LANES))
            for c in range(chans):
                grid = acc[c * TABLE_ROWS : (c + 1) * TABLE_ROWS, :]
                at_cos = jnp.take_along_axis(grid, cos_index, axis=1)
                at_sin = jnp.take_along_axis(grid, sin_index, axis=1)
                re_value = jnp.where(in_sine, at_sin, at_cos) * re_weight
                im_value = jnp.where(in_sine, at_cos, at_sin) * im_weight
                real = jnp.sum(re_value, axis=0, keepdims=True).astype(jnp.bfloat16)
                imag = jnp.sum(im_value, axis=0, keepdims=True).astype(jnp.bfloat16)
                for k in range(0, LANES, cells):
                    out_ref[(start + k) // cells, c : c + 1, :] = real[:, k : k + cells]
                    out_ref[(start + k) // cells, chans + c : chans + c + 1, :] = imag[:, k : k + cells]

    def body(me_ref, tiles_ref, kernel_ref, partial_ref, l_ref, m_ref, uv_ref, sky_ref, out_ref, cube, acc):
        b, j = pl.program_id(0), pl.program_id(1)
        weights = kernel_ref[...].reshape(depth, width)
        term = jnp.dot(tiles_ref[0, 0], weights, preferred_element_type=jnp.float32)

        @pl.when(j == 0)
        def _():
            cube[...] = partial_ref[0] + term

        @pl.when(j > 0)
        def _():
            cube[...] = cube[...] + term

        @pl.when((b == 0) & (j == 0))
        def _():
            acc[...] = jnp.zeros(acc.shape, jnp.float32)

        @pl.when(j == sources - 1)
        def _():
            sky = cube[...]
            sky_ref[:, pl.ds(b, 1), :] = sky[:, None, :]
            low = sky.astype(jnp.bfloat16).astype(jnp.float32)
            waves = l_ref[...][None] * low[:, None, :]
            waves = waves.reshape(chans * TABLE_ROWS, width).astype(jnp.bfloat16)
            acc[...] += lax.dot_general(
                waves, m_ref[...], (((1,), (1,)), ((), ())), preferred_element_type=jnp.float32
            )

        @pl.when((b == blocks - 1) & (j == sources - 1))
        def _():
            select(acc, uv_ref, out_ref)

    def source(me, j):
        return lax.rem(me[0] - j - 1 + snap_count, snap_count)

    return pl.pallas_call(
        body,
        out_shape=(
            jax.ShapeDtypeStruct((chans, blocks, width), jnp.float32),
            jax.ShapeDtypeStruct((owners, 2 * chans, cells), jnp.bfloat16),
        ),
        grid_spec=pltpu.PrefetchScalarGridSpec(
            num_scalar_prefetch=1,
            grid=(blocks, sources),
            in_specs=[
                pl.BlockSpec((1, 1, chans, depth), lambda b, j, me: (j, b, 0, 0)),
                pl.BlockSpec((local_snaps, 1, pix, width), lambda b, j, me: (source(me, j), b, 0, 0)),
                pl.BlockSpec((1, chans, width), lambda b, j, me: (b, 0, 0)),
                pl.BlockSpec((TABLE_ROWS, width), lambda b, j, me: (0, b)),
                pl.BlockSpec((LANES, width), lambda b, j, me: (0, b)),
                pl.BlockSpec((2, modes), lambda b, j, me: (0, 0)),
            ],
            out_specs=(
                pl.BlockSpec((chans, blocks, width), lambda b, j, me: (0, 0, 0)),
                pl.BlockSpec((owners, 2 * chans, cells), lambda b, j, me: (0, 0, 0)),
            ),
            scratch_shapes=[
                pltpu.VMEM((chans, width), jnp.float32),
                pltpu.VMEM((chans * TABLE_ROWS, LANES), jnp.float32),
            ],
        ),
        name="uv_part",
    )(me, other_tiles, kernel, partial, l_table, m_table, mode_uv)


def per_device(snap_tiles, beam_gain, kernel, tile_map, pixel_lm, mode_uv):
    snap_count = lax.axis_size("snap")
    chan_count = lax.axis_size("chan")
    me = lax.axis_index("snap").reshape(1).astype(jnp.int32)
    chans = snap_tiles.shape[1]
    length = chans * chan_count
    modes = mode_uv.shape[1]
    cells = modes // (snap_count * chan_count)
    pixel_total = pixel_lm.shape[1] * snap_count

    sent = gather_tiles(me, tile_map, snap_tiles, beam_gain, (1, snap_count - 1), snap_count)
    received = [
        lax.ppermute(sent[j], "snap", [(i, (i + j + 1) % snap_count) for i in range(snap_count)])[None]
        for j in range(snap_count - 1)
    ]
    own_tiles = gather_tiles(me, tile_map, snap_tiles, beam_gain, (0, 1), snap_count)[0]
    partial, l_table, m_table = own_part(me, own_tiles, kernel, pixel_lm)
    others = received[0] if len(received) == 1 else jnp.concatenate(received)
    sky, spread = uv_part(
        me, others, kernel, partial, l_table, m_table, mode_uv, snap_count, cells, 1.0 / math.sqrt(pixel_total)
    )
    regrouped = lax.all_to_all(spread, ("snap", "chan"), 0, 0, tiled=True)
    columns = regrouped.reshape(snap_count * length * 2, cells)
    matrix = delay_matrix(length).reshape(2, chan_count, chans, 2 * length).transpose(1, 0, 2, 3)
    matrix = np.concatenate([matrix.reshape(2 * length, 2 * length)] * snap_count)
    high = matrix.astype(jnp.bfloat16)
    low = (matrix - high.astype(np.float64)).astype(jnp.bfloat16)

    def transform(part):
        return lax.dot_general(
            columns, jnp.asarray(part), (((0,), (0,)), ((), ())), preferred_element_type=jnp.float32
        )

    delay = (transform(high) + transform(low)).reshape(cells, 2, length)
    return (sky.transpose(1, 0, 2), delay.transpose(1, 2, 0))


def solution(mesh):
    return jax.shard_map(
        per_device,
        mesh=mesh,
        in_specs=(
            P("snap", "chan", None, None),
            P("snap", None, None),
            P(None, "snap", None, None),
            P(),
            P(None, "snap"),
            P(),
        ),
        out_specs=(P("snap", "chan", None), P(None, None, ("snap", "chan"))),
        check_vma=False,
    )
```

```python
import math

import jax
import jax.numpy as jnp
import numpy as np
from jax import lax
from jax.experimental import pallas as pl
from jax.experimental.pallas import tpu as pltpu
from jax.sharding import PartitionSpec as P

LANES = 128
SUBLANES = 8
GROUP = 4
UV_MAX = 32
SINE_ROW = 40
TABLE_ROWS = SINE_ROW + UV_MAX

SMEM = pl.BlockSpec(memory_space=pltpu.SMEM)
VMEM = pl.BlockSpec(memory_space=pltpu.VMEM)
ANY = pl.BlockSpec(memory_space=pl.ANY)


def padded(chans):
    return -(-chans // SUBLANES) * SUBLANES


def delay_matrix(length):
    index = np.arange(length)
    window = 0.54 - 0.46 * np.cos(index * (2.0 * math.pi / (length - 1)))
    phase = (index[:, None] * index[None, :] % length) * (2.0 * math.pi / length)
    scale = window[:, None] / math.sqrt(length)
    cosine, sine = np.cos(phase) * scale, np.sin(phase) * scale
    return np.stack([np.stack([cosine, -sine], 1), np.stack([sine, cosine], 1)])


def cos_turns(angle):
    r = angle - jnp.round(angle)
    square = r * r
    series = jnp.float32(0.0)
    for power in (11, 9, 7, 5, 3, 1):
        term = math.pi**power / math.factorial(power) * (-1.0) ** (power // 2)
        series = series * square + term
    sine = series * r
    return 1.0 - 2.0 * sine * sine


def table(coord):
    row = lax.broadcasted_iota(jnp.int32, (TABLE_ROWS, coord.shape[1]), 0)
    is_sine = row >= SINE_ROW
    k = jnp.where(is_sine, row - (SINE_ROW - 1), row).astype(jnp.float32)
    value = cos_turns(k * coord - jnp.where(is_sine, 0.25, 0.0))
    return jnp.where((row > UV_MAX) & (row < SINE_ROW), 0.0, value)


def tile_scratch(snap_tiles, blocks):
    local_snaps, chans, tiles, pix = snap_tiles.shape
    pitch = tiles + SUBLANES
    return [
        pltpu.VMEM(snap_tiles.shape, jnp.bfloat16),
        pltpu.SemaphoreType.DMA((local_snaps,)),
        *[pltpu.VMEM((chans * pitch, pix), jnp.float32)] * 2,
        *[pltpu.VMEM((blocks * chans, pix), jnp.float32)] * 2,
    ]


def tile_copies(tiles_ref, buffer, sems):
    return [
        pltpu.make_async_copy(tiles_ref.at[s], buffer.at[s], sems.at[s]) for s in range(buffer.shape[0])
    ]


def collect(copies, own, dests, map_ref, buffer, beam_ref, spread, stage, outs):
    local_snaps, chans, tiles, pix = buffer.shape
    blocks = outs[0].shape[0] // chans
    pitch = tiles + SUBLANES
    for s in range(local_snaps):
        if copies:
            copies[s].wait()
        wide = spread[s % 2]
        for c in range(chans):
            wide[c * pitch : c * pitch + tiles, :] = buffer[s, c].astype(jnp.float32) * beam_ref[s]
        for n, (dest, out) in enumerate(zip(dests, outs)):
            rows = stage[(s + n) % 2]
            for b in range(blocks):
                t = map_ref[own * local_snaps + s, dest * blocks + b]
                rows[b * chans : (b + 1) * chans, :] = wide[pl.ds(t, chans, stride=pitch), :]
            out[:, s * pix : (s + 1) * pix] = rows[...].astype(jnp.bfloat16)


def gather_tiles(me, tile_map, snap_tiles, beam_gain, snap_count):
    local_snaps, chans, tiles, pix = snap_tiles.shape
    blocks = tile_map.shape[1] // snap_count

    def body(me_ref, map_ref, tiles_ref, beam_ref, *rest):
        outs, (buffer, sems, *work) = rest[: snap_count - 1], rest[snap_count - 1 :]
        copies = tile_copies(tiles_ref, buffer, sems)
        for copy in copies:
            copy.start()
        own = me_ref[0]
        dests = [lax.rem(own + j, snap_count) for j in range(1, snap_count)]
        collect(copies, own, dests, map_ref, buffer, beam_ref, work[:2], work[2:], outs)

    return pl.pallas_call(
        body,
        out_shape=[jax.ShapeDtypeStruct((blocks * chans, local_snaps * pix), jnp.bfloat16)] * (snap_count - 1),
        in_specs=[SMEM, SMEM, ANY, VMEM],
        out_specs=[VMEM] * (snap_count - 1),
        scratch_shapes=tile_scratch(snap_tiles, blocks),
        name="gather_tiles",
    )(me, tile_map, snap_tiles, beam_gain)


def kernel_copies(kernel_ref, slots, sems, sources, local_snaps):
    groups = kernel_ref.shape[1] // GROUP
    copies = []
    for g in range(groups):
        for source in sources:
            n = len(copies) % slots.shape[0]
            copies.append(
                pltpu.make_async_copy(
                    kernel_ref.at[pl.ds(source * local_snaps, local_snaps), pl.ds(g * GROUP, GROUP)],
                    slots.at[n],
                    sems.at[n],
                )
            )
    return copies


def kernel_scratch(kernel, local_snaps, items):
    _, _, pix, width = kernel.shape
    slots = min(items, 4)
    return [
        pltpu.VMEM((slots, local_snaps, GROUP, pix, width), jnp.bfloat16),
        pltpu.SemaphoreType.DMA((slots,)),
    ]


def group_term(tiles, slot, i, chans):
    local_snaps, _, pix, width = slot.shape
    weights = slot[:, i].reshape(local_snaps * pix, width)
    term = jnp.dot(tiles, weights, preferred_element_type=jnp.float32)
    return term[i * chans : (i + 1) * chans]


def own_part(me, tile_map, snap_tiles, beam_gain, kernel, pixel_lm, snap_count):
    local_snaps, chans, tiles, pix = snap_tiles.shape
    blocks, width = kernel.shape[1], kernel.shape[3]
    groups = blocks // GROUP
    pixels = blocks * width

    def body(me_ref, map_ref, tiles_ref, beam_ref, kernel_ref, lm_ref, cube_ref, l_ref, m_ref, *rest):
        slots, kernel_sems, gathered, buffer, sems, *work = rest
        own = me_ref[0]
        copies = tile_copies(tiles_ref, buffer, sems)
        for copy in copies:
            copy.start()
        weights = kernel_copies(kernel_ref, slots, kernel_sems, [own], local_snaps)
        for copy in weights[: slots.shape[0]]:
            copy.start()
        m_ref[TABLE_ROWS:, :] = jnp.zeros((LANES - TABLE_ROWS, pixels), jnp.bfloat16)
        for b in range(blocks):
            part = slice(b * width, (b + 1) * width)
            l_ref[:, part] = table(lm_ref[0:1, part])
            m_ref[:TABLE_ROWS, part] = table(lm_ref[1:2, part]).astype(jnp.bfloat16)
        collect(copies, own, [own], map_ref, buffer, beam_ref, work[:2], work[2:], [gathered])
        rows = GROUP * chans
        for g in range(groups):
            n = g % slots.shape[0]
            weights[g].wait()
            group_tiles = gathered[g * rows : (g + 1) * rows, :]
            for i in range(GROUP):
                start = g * rows + i * chans
                cube_ref[start : start + chans, :] = group_term(group_tiles, slots.at[n], i, chans)
            if g + slots.shape[0] < groups:
                weights[g + slots.shape[0]].start()

    return pl.pallas_call(
        body,
        out_shape=(
            jax.ShapeDtypeStruct((blocks * chans, width), jnp.float32),
            jax.ShapeDtypeStruct((TABLE_ROWS, pixels), jnp.float32),
            jax.ShapeDtypeStruct((LANES, pixels), jnp.bfloat16),
        ),
        in_specs=[SMEM, SMEM, ANY, VMEM, ANY, VMEM],
        out_specs=(VMEM, VMEM, VMEM),
        scratch_shapes=[
            *kernel_scratch(kernel, local_snaps, groups),
            pltpu.VMEM((blocks * chans, local_snaps * pix), jnp.bfloat16),
            *tile_scratch(snap_tiles, blocks),
        ],
        name="own_part",
    )(me, tile_map, snap_tiles, beam_gain, kernel, pixel_lm)


def uv_part(me, others, kernel, partial, l_table, m_table, columns, chans, cells):
    snap_count = len(others) + 1
    _, blocks, pix, width = kernel.shape
    local_snaps = others[0].shape[1] // pix
    groups = blocks // GROUP
    high = padded(chans)
    cos_rows, sin_rows = (UV_MAX + 1) * high, UV_MAX * high
    owners = columns.shape[1] // (2 * cells)
    chunk = 2 * LANES

    def select(lhs, columns_ref, out_ref):
        lane = lax.broadcasted_iota(jnp.int32, (1, chunk), 1)
        is_imag = lax.rem(lane, 2 * cells) >= cells
        row = lax.broadcasted_iota(jnp.int32, (LANES, chunk), 0)
        for start in range(0, columns.shape[1], chunk):
            u, v = columns_ref[0:1, start : start + chunk], columns_ref[1:2, start : start + chunk]
            sign_u = jnp.where(u < 0, -1.0, 1.0)
            sign_v = jnp.where(v < 0, -1.0, 1.0)
            u, v = jnp.abs(u), jnp.abs(v)
            sin_row = jnp.where(v == 0, -1, v + (SINE_ROW - 1))
            with_cos = jnp.where(row == jnp.where(is_imag, sin_row, v), jnp.where(is_imag, -sign_v, 1.0), 0.0)
            with_sin = jnp.where(
                row == jnp.where(is_imag, v, sin_row), jnp.where(is_imag, -sign_u, -sign_u * sign_v), 0.0
            )
            with_cos, with_sin = with_cos.astype(jnp.bfloat16), with_sin.astype(jnp.bfloat16)
            at_cos = jnp.dot(
                lhs[:cos_rows, :], jnp.concatenate([with_cos, with_cos]), preferred_element_type=jnp.float32
            )
            at_sin = jnp.dot(
                lhs[cos_rows:, :], jnp.concatenate([with_sin, with_sin]), preferred_element_type=jnp.float32
            )
            u = jnp.broadcast_to(u, (high, chunk))
            picked_cos = at_cos[:high]
            picked_sin = jnp.zeros((high, chunk), jnp.float32)
            for k in range(1, UV_MAX + 1):
                hit = u == k
                picked_cos = jnp.where(hit, at_cos[k * high : (k + 1) * high], picked_cos)
                picked_sin = jnp.where(hit, at_sin[(k - 1) * high : k * high], picked_sin)
            value = (picked_cos + picked_sin).astype(jnp.bfloat16)
            for k in range(0, chunk, 2 * cells):
                out_ref[(start + k) // (2 * cells)] = value[:, k : k + 2 * cells]

    def body(me_ref, *rest):
        tiles_refs, rest = rest[: len(others)], rest[len(others) :]
        kernel_ref, partial_ref, l_ref, m_ref, columns_ref, sky_ref, out_ref, slots, sems, low, acc, lhs = rest
        sources = [lax.rem(me_ref[0] + snap_count - j, snap_count) for j in range(1, snap_count)]
        weights = kernel_copies(kernel_ref, slots, sems, sources, local_snaps)
        for copy in weights[: slots.shape[0]]:
            copy.start()
        low[...] = jnp.zeros(low.shape, jnp.float32)
        rows = GROUP * chans
        for g in range(groups):
            sky = [partial_ref[g * rows + i * chans : g * rows + (i + 1) * chans, :] for i in range(GROUP)]
            for j, tiles_ref in enumerate(tiles_refs):
                item = g * len(others) + j
                weights[item].wait()
                group_tiles = tiles_ref[g * rows : (g + 1) * rows, :]
                slot = slots.at[item % slots.shape[0]]
                sky = [sky[i] + group_term(group_tiles, slot, i, chans) for i in range(GROUP)]
                if item + slots.shape[0] < len(weights):
                    weights[item + slots.shape[0]].start()
            for i in range(GROUP):
                b = g * GROUP + i
                part = slice(b * width, (b + 1) * width)
                sky_ref[:, b, :] = sky[i]
                low[i, :chans, :] = sky[i].astype(jnp.bfloat16).astype(jnp.float32)
                value = low[i][None]
                waves = jnp.concatenate(
                    [
                        (l_ref[: UV_MAX + 1, part][:, None, :] * value).reshape(cos_rows, width),
                        (l_ref[SINE_ROW:, part][:, None, :] * value).reshape(sin_rows, width),
                    ]
                ).astype(jnp.bfloat16)
                term = lax.dot_general(
                    waves, m_ref[:, part], (((1,), (1,)), ((), ())), preferred_element_type=jnp.float32
                )
                if b == 0:
                    acc[...] = term
                else:
                    acc[...] += term
        total = acc[...]
        upper = total.astype(jnp.bfloat16)
        lhs[:, :LANES] = upper
        lhs[:, LANES:] = (total - upper.astype(jnp.float32)).astype(jnp.bfloat16)
        select(lhs, columns_ref, out_ref)

    return pl.pallas_call(
        body,
        out_shape=(
            jax.ShapeDtypeStruct((chans, blocks, width), jnp.float32),
            jax.ShapeDtypeStruct((owners, high, 2 * cells), jnp.bfloat16),
        ),
        in_specs=[SMEM, *[VMEM] * len(others), ANY, VMEM, VMEM, VMEM, VMEM],
        out_specs=(VMEM, VMEM),
        scratch_shapes=[
            *kernel_scratch(kernel, local_snaps, groups * len(others)),
            pltpu.VMEM((GROUP, high, width), jnp.float32),
            pltpu.VMEM((cos_rows + sin_rows, LANES), jnp.float32),
            pltpu.VMEM((cos_rows + sin_rows, 2 * LANES), jnp.bfloat16),
        ],
        name="uv_part",
    )(me, *others, kernel, partial, l_table, m_table, columns)


def delay_part(modes, matrix, cells):
    length = matrix.shape[2] // 4

    def body(modes_ref, matrix_ref, out_ref):
        value = modes_ref[...]
        total = jnp.zeros((cells, 2 * length), jnp.float32)
        for part in range(2):
            columns = value[:, part * cells : (part + 1) * cells]
            for piece in range(2):
                total += lax.dot_general(
                    columns,
                    matrix_ref[piece, :, part * 2 * length : (part + 1) * 2 * length],
                    (((0,), (0,)), ((), ())),
                    preferred_element_type=jnp.float32,
                )
        for part in range(2):
            out_ref[part] = total[:, part * length : (part + 1) * length]

    return pl.pallas_call(
        body,
        out_shape=jax.ShapeDtypeStruct((2, cells, length), jnp.float32),
        in_specs=[VMEM, VMEM],
        out_specs=VMEM,
        name="delay_part",
    )(modes, matrix)


def per_device(snap_tiles, beam_gain, kernel, tile_map, pixel_lm, mode_uv):
    snap_count = lax.axis_size("snap")
    chan_count = lax.axis_size("chan")
    me = lax.axis_index("snap").reshape(1).astype(jnp.int32)
    chans = snap_tiles.shape[1]
    high = padded(chans)
    length = chans * chan_count
    owners = snap_count * chan_count
    cells = mode_uv.shape[1] // owners
    pixel_total = pixel_lm.shape[1] * snap_count

    sent = gather_tiles(me, tile_map, snap_tiles, beam_gain, snap_count)
    others = [
        lax.ppermute(part, "snap", [(i, (i + j) % snap_count) for i in range(snap_count)])
        for j, part in enumerate(sent, 1)
    ]
    partial, l_table, m_table = own_part(me, tile_map, snap_tiles, beam_gain, kernel, pixel_lm, snap_count)
    columns = jnp.broadcast_to(mode_uv.reshape(2, owners, 1, cells), (2, owners, 2, cells)).reshape(2, -1)
    sky, spread = uv_part(me, others, kernel, partial, l_table, m_table, columns, chans, cells)
    regrouped = lax.all_to_all(spread, ("snap", "chan"), 0, 0, tiled=True)
    matrix = delay_matrix(length) / math.sqrt(pixel_total)
    matrix = matrix.transpose(1, 0, 2, 3).reshape(chan_count, chans, 4 * length)
    matrix = np.pad(matrix, ((0, 0), (0, high - chans), (0, 0))).reshape(chan_count * high, 4 * length)
    matrix = np.concatenate([matrix] * snap_count)
    upper = matrix.astype(jnp.bfloat16)
    lower = (matrix - upper.astype(np.float64)).astype(jnp.bfloat16)
    delay = delay_part(
        regrouped.reshape(owners * high, 2 * cells), jnp.asarray(np.stack([upper, lower])), cells
    )
    return (sky.transpose(1, 0, 2), delay.transpose(0, 2, 1))


def solution(mesh):
    return jax.shard_map(
        per_device,
        mesh=mesh,
        in_specs=(
            P("snap", "chan", None, None),
            P("snap", None, None),
            P(None, "snap", None, None),
            P(),
            P(None, "snap"),
            P(),
        ),
        out_specs=(P("snap", "chan", None), P(None, None, ("snap", "chan"))),
        check_vma=False,
    )
```

```python
import math

import jax
import jax.numpy as jnp
import numpy as np
from jax import lax
from jax.experimental import pallas as pl
from jax.experimental.pallas import tpu as pltpu
from jax.sharding import PartitionSpec as P

LANES = 128
SUBLANES = 8
GROUP = 4
PARTS = 2
UV_MAX = 32
SINE_ROW = 40
TABLE_ROWS = SINE_ROW + UV_MAX

SMEM = pl.BlockSpec(memory_space=pltpu.SMEM)
VMEM = pl.BlockSpec(memory_space=pltpu.VMEM)
HBM = pl.BlockSpec(memory_space=pltpu.HBM)


def limit(mebibytes):
    return pltpu.CompilerParams(vmem_limit_bytes=mebibytes << 20)


def padded(chans):
    return -(-chans // SUBLANES) * SUBLANES


def delay_matrix(length):
    index = np.arange(length)
    window = 0.54 - 0.46 * np.cos(index * (2.0 * math.pi / (length - 1)))
    phase = (index[:, None] * index[None, :] % length) * (2.0 * math.pi / length)
    scale = window[:, None] / math.sqrt(length)
    cosine, sine = np.cos(phase) * scale, np.sin(phase) * scale
    return np.stack([np.stack([cosine, -sine], 1), np.stack([sine, cosine], 1)])


def cos_turns(angle):
    r = angle - jnp.round(angle)
    square = r * r
    series = jnp.float32(0.0)
    for power in (11, 9, 7, 5, 3, 1):
        term = math.pi**power / math.factorial(power) * (-1.0) ** (power // 2)
        series = series * square + term
    sine = series * r
    return 1.0 - 2.0 * sine * sine


def table(coord):
    row = lax.broadcasted_iota(jnp.int32, (TABLE_ROWS, coord.shape[1]), 0)
    is_sine = row >= SINE_ROW
    k = jnp.where(is_sine, row - (SINE_ROW - 1), row).astype(jnp.float32)
    value = cos_turns(k * coord - jnp.where(is_sine, 0.25, 0.0))
    return jnp.where((row > UV_MAX) & (row < SINE_ROW), 0.0, value)


def tile_scratch(snap_tiles, blocks):
    local_snaps, chans, tiles, pix = snap_tiles.shape
    pitch = tiles + SUBLANES
    return [
        pltpu.VMEM(snap_tiles.shape, jnp.bfloat16),
        pltpu.SemaphoreType.DMA((local_snaps,)),
        *[pltpu.VMEM((chans * pitch, pix), jnp.float32)] * 2,
        *[pltpu.VMEM((blocks * chans, pix), jnp.float32)] * 2,
    ]


def tile_copies(tiles_ref, buffer, sems):
    return [
        pltpu.make_async_copy(tiles_ref.at[s], buffer.at[s], sems.at[s]) for s in range(buffer.shape[0])
    ]


def collect(copies, own, dests, map_ref, buffer, beam_ref, spread, stage, outs):
    local_snaps, chans, tiles, pix = buffer.shape
    blocks = stage[0].shape[0] // chans
    pitch = tiles + SUBLANES
    for s in range(local_snaps):
        if copies:
            copies[s].wait()
        wide = spread[s % 2]
        for c in range(chans):
            wide[c * pitch : c * pitch + tiles, :] = buffer[s, c].astype(jnp.float32) * beam_ref[s]
        for n, (dest, parts) in enumerate(zip(dests, outs)):
            rows = stage[(s + n) % 2]
            for b in range(blocks):
                t = map_ref[own * local_snaps + s, dest * blocks + b]
                rows[b * chans : (b + 1) * chans, :] = wide[pl.ds(t, chans, stride=pitch), :]
            for i, out in enumerate(parts):
                size = out.shape[0]
                out[:, s * pix : (s + 1) * pix] = rows[i * size : (i + 1) * size, :].astype(jnp.bfloat16)


def gather_tiles(tile_map, snap_tiles, beam_gain, snap_count):
    local_snaps, chans, tiles, pix = snap_tiles.shape
    blocks = tile_map.shape[1] // snap_count
    count = (snap_count - 1) * PARTS

    def body(map_ref, tiles_ref, beam_ref, *rest):
        outs, (buffer, sems, *work) = rest[:count], rest[count:]
        copies = tile_copies(tiles_ref, buffer, sems)
        for copy in copies:
            copy.start()
        own = lax.axis_index("snap")
        dests = [lax.rem(own + j, snap_count) for j in range(1, snap_count)]
        outs = [outs[n : n + PARTS] for n in range(0, count, PARTS)]
        collect(copies, own, dests, map_ref, buffer, beam_ref, work[:2], work[2:], outs)

    return pl.pallas_call(
        body,
        out_shape=[pltpu.VMEM((blocks // PARTS * chans, local_snaps * pix), jnp.bfloat16)] * count,
        in_specs=[SMEM, HBM, VMEM],
        out_specs=[VMEM] * count,
        scratch_shapes=tile_scratch(snap_tiles, blocks),
        compiler_params=limit(8),
        name="gather_tiles",
    )(tile_map, snap_tiles, beam_gain)


def kernel_copies(kernel_ref, slots, sems, sources, local_snaps, groups):
    copies = []
    for g in groups:
        for source in sources:
            n = len(copies) % slots.shape[0]
            copies.append(
                pltpu.make_async_copy(
                    kernel_ref.at[pl.ds(source * local_snaps, local_snaps), pl.ds(g * GROUP, GROUP)],
                    slots.at[n],
                    sems.at[n],
                )
            )
    return copies


def kernel_scratch(kernel, local_snaps, items):
    _, _, pix, width = kernel.shape
    slots = min(items, 4)
    return [
        pltpu.VMEM((slots, local_snaps, GROUP, pix, width), jnp.bfloat16),
        pltpu.SemaphoreType.DMA((slots,)),
    ]


def group_term(tiles, slot, i, chans):
    local_snaps, _, pix, width = slot.shape
    weights = slot[:, i].reshape(local_snaps * pix, width)
    term = jnp.dot(tiles, weights, preferred_element_type=jnp.float32)
    return term[i * chans : (i + 1) * chans]


def own_part(tile_map, snap_tiles, beam_gain, kernel, pixel_lm, columns, cells, snap_count):
    local_snaps, chans, tiles, pix = snap_tiles.shape
    blocks, width = kernel.shape[1], kernel.shape[3]
    groups = blocks // GROUP
    pixels = blocks * width

    def body(map_ref, tiles_ref, beam_ref, kernel_ref, lm_ref, columns_ref, cube_ref, l_ref, m_ref, *rest):
        ahead_ref, with_cos_ref, with_sin_ref, slots, kernel_sems, ahead_sem, gathered, buffer, sems, *work = rest
        own = lax.axis_index("snap")
        copies = tile_copies(tiles_ref, buffer, sems)
        for copy in copies:
            copy.start()
        weights = kernel_copies(kernel_ref, slots, kernel_sems, [own], local_snaps, range(groups))
        for copy in weights[: slots.shape[0]]:
            copy.start()
        m_ref[TABLE_ROWS:, :] = jnp.zeros((LANES - TABLE_ROWS, pixels), jnp.bfloat16)
        for b in range(blocks):
            part = slice(b * width, (b + 1) * width)
            l_ref[:, part] = table(lm_ref[0:1, part])
            m_ref[:TABLE_ROWS, part] = table(lm_ref[1:2, part]).astype(jnp.bfloat16)
        source = lax.rem(own + snap_count - 1, snap_count)
        ahead = pltpu.make_async_copy(
            kernel_ref.at[pl.ds(source * local_snaps, local_snaps)], ahead_ref, ahead_sem
        )
        ahead.start()
        collect(copies, own, [own], map_ref, buffer, beam_ref, work[:2], work[2:], [[gathered]])
        rows = GROUP * chans
        for g in range(groups):
            n = g % slots.shape[0]
            weights[g].wait()
            group_tiles = gathered[g * rows : (g + 1) * rows, :]
            for i in range(GROUP):
                start = g * rows + i * chans
                cube_ref[start : start + chans, :] = group_term(group_tiles, slots.at[n], i, chans)
            if g + slots.shape[0] < groups:
                weights[g + slots.shape[0]].start()
        pick_v(columns_ref, with_cos_ref, with_sin_ref, cells)
        ahead.wait()

    return pl.pallas_call(
        body,
        out_shape=(
            pltpu.VMEM((blocks * chans, width), jnp.float32),
            pltpu.VMEM((TABLE_ROWS, pixels), jnp.float32),
            pltpu.VMEM((LANES, pixels), jnp.bfloat16),
            pltpu.VMEM((local_snaps, blocks, pix, width), jnp.bfloat16),
            pltpu.VMEM((LANES, columns.shape[1]), jnp.bfloat16),
            pltpu.VMEM((LANES, columns.shape[1]), jnp.bfloat16),
        ),
        in_specs=[SMEM, HBM, VMEM, HBM, VMEM, VMEM],
        out_specs=(VMEM,) * 6,
        scratch_shapes=[
            *kernel_scratch(kernel, local_snaps, groups),
            pltpu.SemaphoreType.DMA,
            pltpu.VMEM((blocks * chans, local_snaps * pix), jnp.bfloat16),
            *tile_scratch(snap_tiles, blocks),
        ],
        compiler_params=limit(24),
        name="own_part",
    )(tile_map, snap_tiles, beam_gain, kernel, pixel_lm, columns)


def pick_v(columns_ref, with_cos_ref, with_sin_ref, cells):
    chunk = 2 * LANES
    lane = lax.broadcasted_iota(jnp.int32, (1, chunk), 1)
    row = lax.broadcasted_iota(jnp.int32, (LANES, chunk), 0)
    for start in range(0, columns_ref.shape[1], chunk):
        part = slice(start, start + chunk)
        is_imag = lax.rem(lane, 2 * cells) >= cells
        u, v = columns_ref[0:1, part], columns_ref[1:2, part]
        sign_u = jnp.where(u < 0, -1.0, 1.0)
        sign_v = jnp.where(v < 0, -1.0, 1.0)
        v = jnp.abs(v)
        sin_row = jnp.where(v == 0, -1, v + (SINE_ROW - 1))
        with_cos = jnp.where(row == jnp.where(is_imag, sin_row, v), jnp.where(is_imag, -sign_v, 1.0), 0.0)
        with_sin = jnp.where(
            row == jnp.where(is_imag, v, sin_row), jnp.where(is_imag, -sign_u, -sign_u * sign_v), 0.0
        )
        with_cos_ref[:, part] = with_cos.astype(jnp.bfloat16)
        with_sin_ref[:, part] = with_sin.astype(jnp.bfloat16)


def uv_part(others, kernel, ahead, partial, l_table, m_table, first_group, chans, begun=None, picks=None, cells=0):
    snap_count = len(others) + 1
    _, blocks, pix, width = kernel.shape
    local_snaps = others[0].shape[1] // pix
    rows = GROUP * chans
    groups = range(first_group, first_group + others[0].shape[0] // rows)
    high = padded(chans)
    cos_rows, sin_rows = (UV_MAX + 1) * high, UV_MAX * high
    later = len(others) - 1
    last = begun is not None

    def select(lhs, columns_ref, with_cos_ref, with_sin_ref, out_ref):
        chunk = 2 * LANES
        for start in range(0, columns_ref.shape[1], chunk):
            part = slice(start, start + chunk)
            with_cos, with_sin = with_cos_ref[:, part], with_sin_ref[:, part]
            at_cos = jnp.dot(
                lhs[:cos_rows, :], jnp.concatenate([with_cos, with_cos]), preferred_element_type=jnp.float32
            )
            at_sin = jnp.dot(
                lhs[cos_rows:, :], jnp.concatenate([with_sin, with_sin]), preferred_element_type=jnp.float32
            )
            u = jnp.broadcast_to(jnp.abs(columns_ref[0:1, part]), (high, chunk))
            picked_cos = at_cos[:high]
            picked_sin = jnp.zeros((high, chunk), jnp.float32)
            for k in range(1, UV_MAX + 1):
                hit = u == k
                picked_cos = jnp.where(hit, at_cos[k * high : (k + 1) * high], picked_cos)
                picked_sin = jnp.where(hit, at_sin[(k - 1) * high : k * high], picked_sin)
            value = (picked_cos + picked_sin).astype(jnp.bfloat16)
            for k in range(0, chunk, 2 * cells):
                out_ref[(start + k) // (2 * cells)] = value[:, k : k + 2 * cells]

    def body(*rest):
        tiles_refs, rest = rest[: len(others)], rest[len(others) :]
        kernel_ref, ahead_ref, partial_ref, l_ref, m_ref, *rest = rest
        if last:
            begun_cube, begun_acc, columns_ref, with_cos_ref, with_sin_ref, sky_ref, out_ref, low, acc, lhs, *rest = rest
        else:
            cube_ref, acc, low, *rest = rest
        if later:
            slots, sems = rest
            own = lax.axis_index("snap")
            sources = [lax.rem(own + snap_count - j, snap_count) for j in range(2, snap_count)]
            weights = kernel_copies(kernel_ref, slots, sems, sources, local_snaps, groups)
            for copy in weights[: slots.shape[0]]:
                copy.start()
        low[...] = jnp.zeros(low.shape, jnp.float32)
        if last:
            for b in range(first_group * GROUP):
                sky_ref[:, b, :] = begun_cube[b * chans : (b + 1) * chans, :]
        for n, g in enumerate(groups):
            sky = [partial_ref[g * rows + i * chans : g * rows + (i + 1) * chans, :] for i in range(GROUP)]
            near = ahead_ref.at[:, g * GROUP : (g + 1) * GROUP]
            group_tiles = tiles_refs[0][n * rows : (n + 1) * rows, :]
            sky = [sky[i] + group_term(group_tiles, near, i, chans) for i in range(GROUP)]
            for j in range(later):
                item = n * later + j
                weights[item].wait()
                group_tiles = tiles_refs[j + 1][n * rows : (n + 1) * rows, :]
                slot = slots.at[item % slots.shape[0]]
                sky = [sky[i] + group_term(group_tiles, slot, i, chans) for i in range(GROUP)]
                if item + slots.shape[0] < len(weights):
                    weights[item + slots.shape[0]].start()
            for i in range(GROUP):
                b = g * GROUP + i
                part = slice(b * width, (b + 1) * width)
                if last:
                    sky_ref[:, b, :] = sky[i]
                else:
                    cube_ref[b * chans : (b + 1) * chans, :] = sky[i]
                low[i, :chans, :] = sky[i].astype(jnp.bfloat16).astype(jnp.float32)
                value = low[i][None]
                waves = jnp.concatenate(
                    [
                        (l_ref[: UV_MAX + 1, part][:, None, :] * value).reshape(cos_rows, width),
                        (l_ref[SINE_ROW:, part][:, None, :] * value).reshape(sin_rows, width),
                    ]
                ).astype(jnp.bfloat16)
                term = lax.dot_general(
                    waves, m_ref[:, part], (((1,), (1,)), ((), ())), preferred_element_type=jnp.float32
                )
                if n or i:
                    acc[...] += term
                elif last:
                    acc[...] = begun_acc[...] + term
                else:
                    acc[...] = term
        if last:
            total = acc[...]
            upper = total.astype(jnp.bfloat16)
            lhs[:, :LANES] = upper
            lhs[:, LANES:] = (total - upper.astype(jnp.float32)).astype(jnp.bfloat16)
            select(lhs, columns_ref, with_cos_ref, with_sin_ref, out_ref)

    grid_shape = (cos_rows + sin_rows, LANES)
    scratch = [pltpu.VMEM((GROUP, high, width), jnp.float32)]
    operands = [*others, kernel, ahead, partial, l_table, m_table]
    if last:
        columns, with_cos, with_sin = picks
        operands += [*begun, columns, with_cos, with_sin]
        out_shape = (
            pltpu.VMEM((chans, blocks, width), jnp.float32),
            pltpu.VMEM((columns.shape[1] // (2 * cells), high, 2 * cells), jnp.bfloat16),
        )
        scratch += [pltpu.VMEM(grid_shape, jnp.float32), pltpu.VMEM((cos_rows + sin_rows, 2 * LANES), jnp.bfloat16)]
    else:
        out_shape = (
            pltpu.VMEM((groups.stop * rows, width), jnp.float32),
            pltpu.VMEM(grid_shape, jnp.float32),
        )
    if later:
        scratch += kernel_scratch(kernel, local_snaps, len(groups) * later)
    return pl.pallas_call(
        body,
        out_shape=out_shape,
        in_specs=[HBM if operand is kernel else VMEM for operand in operands],
        out_specs=(VMEM, VMEM),
        scratch_shapes=scratch,
        compiler_params=limit(24 if later else 12),
        name="uv_last" if last else "uv_first",
    )(*operands)


def delay_part(modes, matrix, cells):
    length = matrix.shape[2] // 4

    def body(modes_ref, matrix_ref, out_ref):
        value = modes_ref[...]
        total = jnp.zeros((cells, 2 * length), jnp.float32)
        for part in range(2):
            columns = value[:, part * cells : (part + 1) * cells]
            for piece in range(2):
                total += lax.dot_general(
                    columns,
                    matrix_ref[piece, :, part * 2 * length : (part + 1) * 2 * length],
                    (((0,), (0,)), ((), ())),
                    preferred_element_type=jnp.float32,
                )
        for part in range(2):
            out_ref[part] = total[:, part * length : (part + 1) * length]

    return pl.pallas_call(
        body,
        out_shape=jax.ShapeDtypeStruct((2, cells, length), jnp.float32),
        in_specs=[VMEM, VMEM],
        out_specs=VMEM,
        compiler_params=limit(8),
        name="delay_part",
    )(modes, matrix)


def per_device(snap_tiles, beam_gain, kernel, tile_map, pixel_lm, mode_uv):
    snap_count = lax.axis_size("snap")
    chan_count = lax.axis_size("chan")
    chans = snap_tiles.shape[1]
    high = padded(chans)
    length = chans * chan_count
    owners = snap_count * chan_count
    cells = mode_uv.shape[1] // owners
    pixel_total = pixel_lm.shape[1] * snap_count

    snap_tiles, kernel, tile_map = (
        pltpu.with_memory_space_constraint(value, pltpu.HBM) for value in (snap_tiles, kernel, tile_map)
    )
    sent = gather_tiles(tile_map, snap_tiles, pltpu.with_memory_space_constraint(beam_gain, pltpu.HBM), snap_count)
    others = [
        lax.ppermute(part, "snap", [(i, (i + n // PARTS + 1) % snap_count) for i in range(snap_count)])
        for n, part in enumerate(sent)
    ]
    columns = jnp.broadcast_to(mode_uv.reshape(2, owners, 1, cells), (2, owners, 2, cells)).reshape(2, -1)
    partial, l_table, m_table, ahead, *picks = own_part(
        tile_map, snap_tiles, beam_gain, kernel, pixel_lm, columns, cells, snap_count
    )
    shared = (kernel, ahead, partial, l_table, m_table)
    begun = uv_part(others[0::PARTS], *shared, 0, chans)
    half = kernel.shape[1] // GROUP // PARTS
    sky, spread = uv_part(others[1::PARTS], *shared, half, chans, begun, (columns, *picks), cells)
    regrouped = lax.all_to_all(spread, ("snap", "chan"), 0, 0, tiled=True)
    matrix = delay_matrix(length) / math.sqrt(pixel_total)
    matrix = matrix.transpose(1, 0, 2, 3).reshape(chan_count, chans, 4 * length)
    matrix = np.pad(matrix, ((0, 0), (0, high - chans), (0, 0))).reshape(chan_count * high, 4 * length)
    matrix = np.concatenate([matrix] * snap_count)
    upper = matrix.astype(jnp.bfloat16)
    lower = (matrix - upper.astype(np.float64)).astype(jnp.bfloat16)
    delay = delay_part(
        regrouped.reshape(owners * high, 2 * cells), jnp.asarray(np.stack([upper, lower])), cells
    )
    return (sky.transpose(1, 0, 2), delay.transpose(0, 2, 1))


def solution(mesh):
    return jax.shard_map(
        per_device,
        mesh=mesh,
        in_specs=(
            P("snap", "chan", None, None),
            P("snap", None, None),
            P(None, "snap", None, None),
            P(),
            P(None, "snap"),
            P(),
        ),
        out_specs=(P("snap", "chan", None), P(None, None, ("snap", "chan"))),
        check_vma=False,
    )
```

```python
import math

import jax
import jax.numpy as jnp
import numpy as np
from jax import lax
from jax.experimental import pallas as pl
from jax.experimental.pallas import tpu as pltpu
from jax.sharding import PartitionSpec as P

LANES = 128
SUBLANES = 8
GROUP = 4
PARTS = 2
UV_MAX = 32
SINE_ROW = 40
TABLE_ROWS = SINE_ROW + UV_MAX

VMEM = pl.BlockSpec(memory_space=pltpu.VMEM)
HBM = pl.BlockSpec(memory_space=pltpu.HBM)


def limit(mebibytes):
    return pltpu.CompilerParams(vmem_limit_bytes=mebibytes << 20)


def padded(chans):
    return -(-chans // SUBLANES) * SUBLANES


def delay_matrix(length):
    index = np.arange(length)
    window = 0.54 - 0.46 * np.cos(index * (2.0 * math.pi / (length - 1)))
    phase = (index[:, None] * index[None, :] % length) * (2.0 * math.pi / length)
    scale = window[:, None] / math.sqrt(length)
    cosine, sine = np.cos(phase) * scale, np.sin(phase) * scale
    return np.stack([np.stack([cosine, -sine], 1), np.stack([sine, cosine], 1)])


def cos_turns(angle):
    r = angle - jnp.round(angle)
    square = r * r
    series = jnp.float32(0.0)
    for power in (11, 9, 7, 5, 3, 1):
        term = math.pi**power / math.factorial(power) * (-1.0) ** (power // 2)
        series = series * square + term
    sine = series * r
    return 1.0 - 2.0 * sine * sine


def table(coord):
    shape = (SUBLANES, coord.shape[1])
    row = lax.broadcasted_iota(jnp.int32, shape, 0)
    steps = UV_MAX // SUBLANES
    fine = row.astype(jnp.float32) * coord
    fine_cos, fine_sin = cos_turns(fine), cos_turns(fine - 0.25)
    coarse_k = ((lax.rem(row, steps) + 1) * SUBLANES).astype(jnp.float32)
    coarse = cos_turns(coarse_k * coord - jnp.where(row < steps, 0.0, 0.25))
    cosines, sines = [fine_cos], [fine_sin]
    for a in range(1, steps + 1):
        step_cos, step_sin = coarse[a - 1 : a], coarse[steps + a - 1 : steps + a]
        cosines.append(step_cos * fine_cos - step_sin * fine_sin)
        sines.append(step_sin * fine_cos + step_cos * fine_sin)
    cosines[-1] = jnp.where(row > 0, 0.0, cosines[-1])
    sines[0] = jnp.where(row > 0, sines[0], sines.pop())
    return jnp.concatenate([*cosines, *sines])


def tile_scratch(tile_map, snap_tiles, blocks):
    local_snaps, chans, tiles, pix = snap_tiles.shape
    pitch = tiles + SUBLANES
    return [
        pltpu.SMEM(tile_map.shape, jnp.int32),
        pltpu.VMEM((local_snaps, tiles, pix), jnp.float32),
        pltpu.VMEM(snap_tiles.shape, jnp.bfloat16),
        pltpu.SemaphoreType.DMA((local_snaps + 2,)),
        *[pltpu.VMEM((chans * pitch, pix), jnp.float32)] * 2,
        *[pltpu.VMEM((blocks * chans, pix), jnp.float32)] * 2,
    ]


def tile_copies(sources, map_ref, beam_ref, buffer, sems):
    map_hbm, tiles_hbm, beam_hbm = sources
    snaps = range(buffer.shape[0])
    return [
        pltpu.make_async_copy(map_hbm, map_ref, sems.at[len(snaps)]),
        pltpu.make_async_copy(beam_hbm, beam_ref, sems.at[len(snaps) + 1]),
        *[pltpu.make_async_copy(tiles_hbm.at[s], buffer.at[s], sems.at[s]) for s in snaps],
    ]


def collect(copies, own, dests, map_ref, buffer, beam_ref, spread, stage, outs):
    local_snaps, chans, tiles, pix = buffer.shape
    blocks = stage[0].shape[0] // chans
    pitch = tiles + SUBLANES
    copies[0].wait()
    copies[1].wait()
    for s in range(local_snaps):
        copies[s + 2].wait()
        wide = spread[s % 2]
        for c in range(chans):
            wide[c * pitch : c * pitch + tiles, :] = buffer[s, c].astype(jnp.float32) * beam_ref[s]
        for n, (dest, parts) in enumerate(zip(dests, outs)):
            rows = stage[(s + n) % 2]
            for b in range(blocks):
                t = map_ref[own * local_snaps + s, dest * blocks + b]
                rows[b * chans : (b + 1) * chans, :] = wide[pl.ds(t, chans, stride=pitch), :]
            for i, out in enumerate(parts):
                size = out.shape[0]
                out[:, s * pix : (s + 1) * pix] = rows[i * size : (i + 1) * size, :].astype(jnp.bfloat16)


def gather_tiles(tile_map, snap_tiles, beam_gain, snap_count):
    local_snaps, chans, tiles, pix = snap_tiles.shape
    blocks = tile_map.shape[1] // snap_count
    count = (snap_count - 1) * PARTS

    def body(map_hbm, tiles_hbm, beam_hbm, *rest):
        outs, (map_ref, beam_ref, buffer, sems, *work) = rest[:count], rest[count:]
        copies = tile_copies((map_hbm, tiles_hbm, beam_hbm), map_ref, beam_ref, buffer, sems)
        for copy in copies:
            copy.start()
        own = lax.axis_index("snap")
        dests = [lax.rem(own + j, snap_count) for j in range(1, snap_count)]
        outs = [outs[n : n + PARTS] for n in range(0, count, PARTS)]
        collect(copies, own, dests, map_ref, buffer, beam_ref, work[:2], work[2:], outs)

    return pl.pallas_call(
        body,
        out_shape=[pltpu.VMEM((blocks // PARTS * chans, local_snaps * pix), jnp.bfloat16)] * count,
        in_specs=[HBM, HBM, HBM],
        out_specs=[VMEM] * count,
        scratch_shapes=tile_scratch(tile_map, snap_tiles, blocks),
        compiler_params=limit(8),
        name="gather_tiles",
    )(tile_map, snap_tiles, beam_gain)


def kernel_copies(kernel_ref, slots, sems, sources, local_snaps, groups):
    copies = []
    for g in groups:
        for source in sources:
            n = len(copies) % slots.shape[0]
            copies.append(
                pltpu.make_async_copy(
                    kernel_ref.at[pl.ds(source * local_snaps, local_snaps), pl.ds(g * GROUP, GROUP)],
                    slots.at[n],
                    sems.at[n],
                )
            )
    return copies


def fence(ref):
    @pl.when(lax.axis_index("snap") < 0)
    def _():
        ref[...] = jnp.zeros(ref.shape, ref.dtype)


def ahead_copy(kernel_ref, ahead_ref, sem, first_block, snap_count):
    local_snaps, blocks = ahead_ref.shape[:2]
    source = lax.rem(lax.axis_index("snap") + snap_count - 1, snap_count)
    return pltpu.make_async_copy(
        kernel_ref.at[pl.ds(source * local_snaps, local_snaps), pl.ds(first_block, blocks)], ahead_ref, sem
    )


def kernel_scratch(kernel, local_snaps, items):
    _, _, pix, width = kernel.shape
    slots = min(items, 4)
    return [
        pltpu.VMEM((slots, local_snaps, GROUP, pix, width), jnp.bfloat16),
        pltpu.SemaphoreType.DMA((slots,)),
    ]


def group_term(tiles, slot, i, chans):
    local_snaps, _, pix, width = slot.shape
    weights = slot[:, i].reshape(local_snaps * pix, width)
    term = jnp.dot(tiles, weights, preferred_element_type=jnp.float32)
    return term[i * chans : (i + 1) * chans]


def own_part(tile_map, snap_tiles, beam_gain, kernel, pixel_lm, mode_uv, cells, snap_count):
    local_snaps, chans, tiles, pix = snap_tiles.shape
    blocks, width = kernel.shape[1], kernel.shape[3]
    groups = blocks // GROUP
    pixels = blocks * width
    columns = 2 * mode_uv.shape[1]

    def body(map_hbm, tiles_hbm, beam_hbm, kernel_ref, lm_hbm, uv_hbm, cube_ref, l_ref, m_ref, *rest):
        ahead_ref, columns_ref, with_cos_ref, with_sin_ref, slots, kernel_sems, ahead_sem, gathered, *rest = rest
        lm_ref, uv_ref, own_sems, *rest = rest
        map_ref, beam_ref, buffer, sems, *work = rest
        own = lax.axis_index("snap")
        copies = tile_copies((map_hbm, tiles_hbm, beam_hbm), map_ref, beam_ref, buffer, sems)
        small = [
            pltpu.make_async_copy(lm_hbm, lm_ref, own_sems.at[0]),
            pltpu.make_async_copy(uv_hbm, uv_ref, own_sems.at[1]),
        ]
        for copy in [*small, *copies]:
            copy.start()
        weights = kernel_copies(kernel_ref, slots, kernel_sems, [own], local_snaps, range(groups))
        for copy in weights[: slots.shape[0]]:
            copy.start()
        ahead = ahead_copy(kernel_ref, ahead_ref, ahead_sem, 0, snap_count)
        ahead.start()
        small[0].wait()
        m_ref[TABLE_ROWS:, :] = jnp.zeros((LANES - TABLE_ROWS, pixels), jnp.bfloat16)
        for b in range(blocks):
            part = slice(b * width, (b + 1) * width)
            l_ref[:, part] = table(lm_ref[0:1, part])
            m_ref[:TABLE_ROWS, part] = table(lm_ref[1:2, part]).astype(jnp.bfloat16)
        small[1].wait()
        pick_v(uv_ref, columns_ref, with_cos_ref, with_sin_ref, cells)
        collect(copies, own, [own], map_ref, buffer, beam_ref, work[:2], work[2:], [[gathered]])
        rows = GROUP * chans
        for g in range(groups):
            n = g % slots.shape[0]
            weights[g].wait()
            group_tiles = gathered[g * rows : (g + 1) * rows, :]
            for i in range(GROUP):
                start = g * rows + i * chans
                cube_ref[start : start + chans, :] = group_term(group_tiles, slots.at[n], i, chans)
            if g + slots.shape[0] < groups:
                weights[g + slots.shape[0]].start()
        ahead.wait()

    return pl.pallas_call(
        body,
        out_shape=(
            pltpu.VMEM((blocks * chans, width), jnp.float32),
            pltpu.VMEM((TABLE_ROWS, pixels), jnp.float32),
            pltpu.VMEM((LANES, pixels), jnp.bfloat16),
            pltpu.VMEM((local_snaps, GROUP, pix, width), jnp.bfloat16),
            pltpu.VMEM((2, columns), jnp.int32),
            pltpu.VMEM((LANES, columns), jnp.bfloat16),
            pltpu.VMEM((LANES, columns), jnp.bfloat16),
        ),
        in_specs=[HBM] * 6,
        out_specs=(VMEM,) * 7,
        scratch_shapes=[
            *kernel_scratch(kernel, local_snaps, groups),
            pltpu.SemaphoreType.DMA,
            pltpu.VMEM((blocks * chans, local_snaps * pix), jnp.bfloat16),
            pltpu.VMEM(pixel_lm.shape, jnp.float32),
            pltpu.VMEM(mode_uv.shape, jnp.int32),
            pltpu.SemaphoreType.DMA((2,)),
            *tile_scratch(tile_map, snap_tiles, blocks),
        ],
        compiler_params=limit(24),
        name="own_part",
    )(tile_map, snap_tiles, beam_gain, kernel, pixel_lm, mode_uv)


def pick_v(uv_ref, columns_ref, with_cos_ref, with_sin_ref, cells):
    chunk = 2 * LANES
    lane = lax.broadcasted_iota(jnp.int32, (1, chunk), 1)
    row = lax.broadcasted_iota(jnp.int32, (TABLE_ROWS, chunk), 0)
    for start in range(0, columns_ref.shape[1], chunk):
        part = slice(start, start + chunk)
        is_imag = lax.rem(lane, 2 * cells) >= cells
        modes = uv_ref[:, start // 2 : start // 2 + LANES]
        owned = [modes[:, k : k + cells] for k in range(0, LANES, cells)]
        both = jnp.concatenate([piece for piece in owned for _ in range(2)], axis=1)
        columns_ref[:, part] = both
        u, v = both[0:1], both[1:2]
        sign_u = jnp.where(u < 0, -1.0, 1.0)
        sign_v = jnp.where(v < 0, -1.0, 1.0)
        v = jnp.abs(v)
        sin_row = jnp.where(v == 0, -1, SINE_ROW + lax.rem(v, UV_MAX))
        with_cos = jnp.where(row == jnp.where(is_imag, sin_row, v), jnp.where(is_imag, -sign_v, 1.0), 0.0)
        with_sin = jnp.where(
            row == jnp.where(is_imag, v, sin_row), jnp.where(is_imag, -sign_u, -sign_u * sign_v), 0.0
        )
        empty = jnp.zeros((LANES - TABLE_ROWS, chunk), jnp.float32)
        with_cos_ref[:, part] = jnp.concatenate([with_cos, empty]).astype(jnp.bfloat16)
        with_sin_ref[:, part] = jnp.concatenate([with_sin, empty]).astype(jnp.bfloat16)


def uv_part(others, kernel, ahead, partial, l_table, m_table, first_group, chans, begun=None, picks=None, cells=0):
    snap_count = len(others) + 1
    _, blocks, pix, width = kernel.shape
    local_snaps = others[0].shape[1] // pix
    rows = GROUP * chans
    groups = range(first_group, first_group + others[0].shape[0] // rows)
    high = padded(chans)
    cos_rows, sin_rows = (UV_MAX + 1) * high, UV_MAX * high
    later = len(others) - 1
    last = begun is not None

    def select(lhs, columns_ref, with_cos_ref, with_sin_ref, out_ref):
        chunk = 2 * LANES
        for start in range(0, columns_ref.shape[1], chunk):
            part = slice(start, start + chunk)
            with_cos, with_sin = with_cos_ref[:, part], with_sin_ref[:, part]
            at_cos = jnp.dot(
                lhs[:cos_rows, :], jnp.concatenate([with_cos, with_cos]), preferred_element_type=jnp.float32
            )
            at_sin = jnp.dot(
                lhs[cos_rows:, :], jnp.concatenate([with_sin, with_sin]), preferred_element_type=jnp.float32
            )
            u = jnp.broadcast_to(jnp.abs(columns_ref[0:1, part]), (high, chunk))
            picked_cos = at_cos[:high]
            picked_sin = jnp.zeros((high, chunk), jnp.float32)
            for k in range(1, UV_MAX + 1):
                hit = u == k
                sin_at = k % UV_MAX * high
                picked_cos = jnp.where(hit, at_cos[k * high : (k + 1) * high], picked_cos)
                picked_sin = jnp.where(hit, at_sin[sin_at : sin_at + high], picked_sin)
            value = (picked_cos + picked_sin).astype(jnp.bfloat16)
            for k in range(0, chunk, 2 * cells):
                out_ref[(start + k) // (2 * cells)] = value[:, k : k + 2 * cells]

    def body(*rest):
        tiles_refs, rest = rest[: len(others)], rest[len(others) :]
        kernel_ref, ahead_ref, partial_ref, l_ref, m_ref, *rest = rest
        if last:
            begun_cube, begun_acc, columns_ref, with_cos_ref, with_sin_ref, sky_ref, out_ref, low, acc, lhs, *rest = rest
        else:
            cube_ref, acc, next_ref, low, fetched, fetch_sems, *rest = rest
            following = [
                ahead_copy(kernel_ref, fetched, fetch_sems.at[0], GROUP, snap_count),
                ahead_copy(kernel_ref, next_ref, fetch_sems.at[1], groups.stop * GROUP, snap_count),
            ]
            for copy in following:
                copy.start()
            fence(acc)
        if later:
            slots, sems = rest
            own = lax.axis_index("snap")
            sources = [lax.rem(own + snap_count - j, snap_count) for j in range(2, snap_count)]
            weights = kernel_copies(kernel_ref, slots, sems, sources, local_snaps, groups)
            for copy in weights[: slots.shape[0]]:
                copy.start()
        low[...] = jnp.zeros(low.shape, jnp.float32)
        if last:
            for b in range(first_group * GROUP):
                sky_ref[:, b, :] = begun_cube[b * chans : (b + 1) * chans, :]
        for n, g in enumerate(groups):
            sky = [partial_ref[g * rows + i * chans : g * rows + (i + 1) * chans, :] for i in range(GROUP)]
            near, at = ahead_ref, n * GROUP
            if not last and n > 0:
                near, at = fetched, at - GROUP
                if n == 1:
                    following[0].wait()
            near = near.at[:, at : at + GROUP]
            group_tiles = tiles_refs[0][n * rows : (n + 1) * rows, :]
            sky = [sky[i] + group_term(group_tiles, near, i, chans) for i in range(GROUP)]
            for j in range(later):
                item = n * later + j
                weights[item].wait()
                group_tiles = tiles_refs[j + 1][n * rows : (n + 1) * rows, :]
                slot = slots.at[item % slots.shape[0]]
                sky = [sky[i] + group_term(group_tiles, slot, i, chans) for i in range(GROUP)]
                if item + slots.shape[0] < len(weights):
                    weights[item + slots.shape[0]].start()
            for i in range(GROUP):
                b = g * GROUP + i
                part = slice(b * width, (b + 1) * width)
                if last:
                    sky_ref[:, b, :] = sky[i]
                else:
                    cube_ref[b * chans : (b + 1) * chans, :] = sky[i]
                low[i, :chans, :] = sky[i].astype(jnp.bfloat16).astype(jnp.float32)
                value = low[i][None]
                waves = jnp.concatenate(
                    [
                        (l_ref[: UV_MAX + 1, part][:, None, :] * value).reshape(cos_rows, width),
                        (l_ref[SINE_ROW:, part][:, None, :] * value).reshape(sin_rows, width),
                    ]
                ).astype(jnp.bfloat16)
                term = lax.dot_general(
                    waves, m_ref[:, part], (((1,), (1,)), ((), ())), preferred_element_type=jnp.float32
                )
                if n or i:
                    acc[...] += term
                elif last:
                    acc[...] = begun_acc[...] + term
                else:
                    acc[...] = term
        if last:
            total = acc[...]
            upper = total.astype(jnp.bfloat16)
            lhs[:, :LANES] = upper
            lhs[:, LANES:] = (total - upper.astype(jnp.float32)).astype(jnp.bfloat16)
            select(lhs, columns_ref, with_cos_ref, with_sin_ref, out_ref)
        else:
            following[1].wait()

    grid_shape = (cos_rows + sin_rows, LANES)
    scratch = [pltpu.VMEM((GROUP, high, width), jnp.float32)]
    operands = [*others, kernel, ahead, partial, l_table, m_table]
    if last:
        columns, with_cos, with_sin = picks
        operands += [*begun, columns, with_cos, with_sin]
        out_shape = (
            pltpu.VMEM((chans, blocks, width), jnp.float32),
            pltpu.VMEM((columns.shape[1] // (2 * cells), high, 2 * cells), jnp.bfloat16),
        )
        scratch += [pltpu.VMEM(grid_shape, jnp.float32), pltpu.VMEM((cos_rows + sin_rows, 2 * LANES), jnp.bfloat16)]
    else:
        out_shape = (
            pltpu.VMEM((groups.stop * rows, width), jnp.float32),
            pltpu.VMEM(grid_shape, jnp.float32),
            pltpu.VMEM((local_snaps, blocks - groups.stop * GROUP, pix, width), jnp.bfloat16),
        )
        fetched = (local_snaps, groups.stop * GROUP - GROUP, pix, width)
        scratch += [pltpu.VMEM(fetched, jnp.bfloat16), pltpu.SemaphoreType.DMA((2,))]
    if later:
        scratch += kernel_scratch(kernel, local_snaps, len(groups) * later)
    return pl.pallas_call(
        body,
        out_shape=out_shape,
        in_specs=[HBM if operand is kernel else VMEM for operand in operands],
        out_specs=(VMEM,) * len(out_shape),
        scratch_shapes=scratch,
        compiler_params=limit(24 if later else 12),
        name="uv_last" if last else "uv_first",
    )(*operands)


def delay_part(modes, matrix, cells):
    length = matrix.shape[2] // 4

    def body(modes_ref, matrix_ref, out_ref):
        value = modes_ref[...]
        total = jnp.zeros((cells, 2 * length), jnp.float32)
        for part in range(2):
            columns = value[:, part * cells : (part + 1) * cells]
            for piece in range(2):
                total += lax.dot_general(
                    columns,
                    matrix_ref[piece, :, part * 2 * length : (part + 1) * 2 * length],
                    (((0,), (0,)), ((), ())),
                    preferred_element_type=jnp.float32,
                )
        for part in range(2):
            out_ref[part] = total[:, part * length : (part + 1) * length]

    return pl.pallas_call(
        body,
        out_shape=jax.ShapeDtypeStruct((2, cells, length), jnp.float32),
        in_specs=[VMEM, VMEM],
        out_specs=VMEM,
        compiler_params=limit(8),
        name="delay_part",
    )(modes, matrix)


def per_device(snap_tiles, beam_gain, kernel, tile_map, pixel_lm, mode_uv):
    snap_count = lax.axis_size("snap")
    chan_count = lax.axis_size("chan")
    chans = snap_tiles.shape[1]
    high = padded(chans)
    length = chans * chan_count
    owners = snap_count * chan_count
    cells = mode_uv.shape[1] // owners
    pixel_total = pixel_lm.shape[1] * snap_count

    snap_tiles, beam_gain, kernel, tile_map, pixel_lm, mode_uv = (
        pltpu.with_memory_space_constraint(value, pltpu.HBM)
        for value in (snap_tiles, beam_gain, kernel, tile_map, pixel_lm, mode_uv)
    )
    sent = gather_tiles(tile_map, snap_tiles, beam_gain, snap_count)
    others = [
        lax.ppermute(part, "snap", [(i, (i + n // PARTS + 1) % snap_count) for i in range(snap_count)])
        for n, part in enumerate(sent)
    ]
    partial, l_table, m_table, ahead, *picks = own_part(
        tile_map, snap_tiles, beam_gain, kernel, pixel_lm, mode_uv, cells, snap_count
    )
    shared = (partial, l_table, m_table)
    *begun, ahead_next = uv_part(others[0::PARTS], kernel, ahead, *shared, 0, chans)
    half = kernel.shape[1] // GROUP // PARTS
    sky, spread = uv_part(others[1::PARTS], kernel, ahead_next, *shared, half, chans, begun, picks, cells)
    regrouped = lax.all_to_all(spread, ("snap", "chan"), 0, 0, tiled=True)
    matrix = delay_matrix(length) / math.sqrt(pixel_total)
    matrix = matrix.transpose(1, 0, 2, 3).reshape(chan_count, chans, 4 * length)
    matrix = np.pad(matrix, ((0, 0), (0, high - chans), (0, 0))).reshape(chan_count * high, 4 * length)
    matrix = np.concatenate([matrix] * snap_count)
    upper = matrix.astype(jnp.bfloat16)
    lower = (matrix - upper.astype(np.float64)).astype(jnp.bfloat16)
    delay = delay_part(
        regrouped.reshape(owners * high, 2 * cells), jnp.asarray(np.stack([upper, lower])), cells
    )
    return (sky.transpose(1, 0, 2), delay.transpose(0, 2, 1))


def solution(mesh):
    return jax.shard_map(
        per_device,
        mesh=mesh,
        in_specs=(
            P("snap", "chan", None, None),
            P("snap", None, None),
            P(None, "snap", None, None),
            P(),
            P(None, "snap"),
            P(),
        ),
        out_specs=(P("snap", "chan", None), P(None, None, ("snap", "chan"))),
        check_vma=False,
    )
```

```python
import math

import jax
import jax.numpy as jnp
import numpy as np
from jax import lax
from jax.experimental import pallas as pl
from jax.experimental.pallas import tpu as pltpu
from jax.sharding import PartitionSpec as P

LANES = 128
SUBLANES = 8
GROUP = 4
PARTS = 2
UV_MAX = 32
SINE_ROW = 40
TABLE_ROWS = SINE_ROW + UV_MAX

VMEM = pl.BlockSpec(memory_space=pltpu.VMEM)
HBM = pl.BlockSpec(memory_space=pltpu.HBM)


def limit(mebibytes):
    return pltpu.CompilerParams(vmem_limit_bytes=mebibytes << 20)


def padded(chans):
    return -(-chans // SUBLANES) * SUBLANES


def together(chans):
    return SUBLANES // math.gcd(SUBLANES, chans)


def delay_matrix(length):
    index = np.arange(length)
    window = 0.54 - 0.46 * np.cos(index * (2.0 * math.pi / (length - 1)))
    phase = (index[:, None] * index[None, :] % length) * (2.0 * math.pi / length)
    scale = window[:, None] / math.sqrt(length)
    cosine, sine = np.cos(phase) * scale, np.sin(phase) * scale
    return np.stack([np.stack([cosine, -sine], 1), np.stack([sine, cosine], 1)])


def cos_turns(angle):
    r = angle - jnp.round(angle)
    square = r * r
    series = jnp.float32(0.0)
    for power in (11, 9, 7, 5, 3, 1):
        term = math.pi**power / math.factorial(power) * (-1.0) ** (power // 2)
        series = series * square + term
    sine = series * r
    return 1.0 - 2.0 * sine * sine


def table(coord):
    shape = (SUBLANES, coord.shape[1])
    row = lax.broadcasted_iota(jnp.int32, shape, 0)
    steps = UV_MAX // SUBLANES
    fine = row.astype(jnp.float32) * coord
    fine_cos, fine_sin = cos_turns(fine), cos_turns(fine - 0.25)
    coarse_k = ((lax.rem(row, steps) + 1) * SUBLANES).astype(jnp.float32)
    coarse = cos_turns(coarse_k * coord - jnp.where(row < steps, 0.0, 0.25))
    cosines, sines = [fine_cos], [fine_sin]
    for a in range(1, steps + 1):
        step_cos, step_sin = coarse[a - 1 : a], coarse[steps + a - 1 : steps + a]
        cosines.append(step_cos * fine_cos - step_sin * fine_sin)
        sines.append(step_sin * fine_cos + step_cos * fine_sin)
    cosines[-1] = jnp.where(row > 0, 0.0, cosines[-1])
    sines[0] = jnp.where(row > 0, sines[0], sines.pop())
    return jnp.concatenate([*cosines, *sines])


def tile_scratch(tile_map, snap_tiles, blocks, copies):
    local_snaps, chans, tiles, pix = snap_tiles.shape
    pitch = tiles + SUBLANES
    return [
        pltpu.SMEM(tile_map.shape, jnp.int32),
        pltpu.SemaphoreType.DMA((copies,)),
        *[pltpu.VMEM((chans * pitch, pix), jnp.float32)] * 2,
        *[pltpu.VMEM((blocks * chans, pix), jnp.float32)] * 2,
    ]


def collect(ready, own, dests, map_ref, buffer, beam_ref, spread, stage, outs):
    local_snaps, chans, tiles, pix = buffer.shape
    blocks = stage[0].shape[0] // chans
    pitch = tiles + SUBLANES
    for s in range(local_snaps):
        ready(s)
        wide = spread[s % 2]
        for c in range(chans):
            wide[c * pitch : c * pitch + tiles, :] = buffer[s, c].astype(jnp.float32) * beam_ref[s]
        for n, (dest, parts) in enumerate(zip(dests, outs)):
            rows = stage[(s + n) % 2]
            for b in range(blocks):
                t = map_ref[own * local_snaps + s, dest * blocks + b]
                rows[b * chans : (b + 1) * chans, :] = wide[pl.ds(t, chans, stride=pitch), :]
            for i, out in enumerate(parts):
                size = out.shape[0]
                out[:, s * pix : (s + 1) * pix] = rows[i * size : (i + 1) * size, :].astype(jnp.bfloat16)


def gather_tiles(tile_map, snap_tiles, beam_gain, pixel_lm, mode_uv, snap_count):
    local_snaps, chans, tiles, pix = snap_tiles.shape
    blocks = tile_map.shape[1] // snap_count
    count = (snap_count - 1) * PARTS
    fetched = (snap_tiles, beam_gain, pixel_lm, mode_uv)

    def body(map_hbm, tiles_hbm, beam_hbm, lm_hbm, uv_hbm, *rest):
        outs, (buffer, beam_ref, lm_ref, uv_ref, map_ref, sems, *work) = rest[:count], rest[count:]
        copies = [
            pltpu.make_async_copy(source, target, sems.at[local_snaps + n])
            for n, (source, target) in enumerate(
                [(map_hbm, map_ref), (beam_hbm, beam_ref), (lm_hbm, lm_ref), (uv_hbm, uv_ref)]
            )
        ]
        of_snap = [
            pltpu.make_async_copy(tiles_hbm.at[s], buffer.at[s], sems.at[s]) for s in range(local_snaps)
        ]
        for copy in [*copies[:2], *of_snap, *copies[2:]]:
            copy.start()
        own = lax.axis_index("snap")
        dests = [lax.rem(own + j, snap_count) for j in range(1, snap_count)]
        outs = [outs[n : n + PARTS] for n in range(0, count, PARTS)]

        def ready(s):
            if s == 0:
                copies[0].wait()
                copies[1].wait()
            of_snap[s].wait()

        collect(ready, own, dests, map_ref, buffer, beam_ref, work[:2], work[2:], outs)
        copies[2].wait()
        copies[3].wait()

    return pl.pallas_call(
        body,
        out_shape=[
            *[pltpu.VMEM((blocks // PARTS * chans, local_snaps * pix), jnp.bfloat16)] * count,
            *[pltpu.VMEM(value.shape, value.dtype) for value in fetched],
        ],
        in_specs=[HBM] * 5,
        out_specs=[VMEM] * (count + len(fetched)),
        scratch_shapes=tile_scratch(tile_map, snap_tiles, blocks, local_snaps + 4),
        compiler_params=limit(8),
        name="gather_tiles",
    )(tile_map, *fetched)


def kernel_copies(kernel_ref, slots, sems, sources, local_snaps, groups):
    copies = []
    for g in groups:
        for source in sources:
            n = len(copies) % slots.shape[0]
            copies.append(
                pltpu.make_async_copy(
                    kernel_ref.at[pl.ds(source * local_snaps, local_snaps), pl.ds(g * GROUP, GROUP)],
                    slots.at[n],
                    sems.at[n],
                )
            )
    return copies


def fence(ref):
    @pl.when(lax.axis_index("snap") < 0)
    def _():
        ref[...] = jnp.zeros(ref.shape, ref.dtype)


def ahead_copy(kernel_ref, ahead_ref, sem, first_block, snap_count):
    local_snaps, blocks = ahead_ref.shape[:2]
    source = lax.rem(lax.axis_index("snap") + snap_count - 1, snap_count)
    return pltpu.make_async_copy(
        kernel_ref.at[pl.ds(source * local_snaps, local_snaps), pl.ds(first_block, blocks)], ahead_ref, sem
    )


def kernel_scratch(kernel, local_snaps, items):
    _, _, pix, width = kernel.shape
    slots = min(items, 4)
    return [
        pltpu.VMEM((slots, local_snaps, GROUP, pix, width), jnp.bfloat16),
        pltpu.SemaphoreType.DMA((slots,)),
    ]


def group_term(tiles, slot, i, chans):
    local_snaps, _, pix, width = slot.shape
    weights = slot[:, i].reshape(local_snaps * pix, width)
    term = jnp.dot(tiles, weights, preferred_element_type=jnp.float32)
    return term[i * chans : (i + 1) * chans]


def own_part(tile_map, snap_tiles, beam_gain, kernel, pixel_lm, mode_uv, cells, snap_count):
    local_snaps, chans, tiles, pix = snap_tiles.shape
    blocks, width = kernel.shape[1], kernel.shape[3]
    groups = blocks // GROUP
    pixels = blocks * width
    columns = 2 * mode_uv.shape[1]

    def body(map_hbm, buffer, beam_ref, kernel_ref, lm_ref, uv_ref, cube_ref, l_ref, m_ref, *rest):
        ahead_ref, columns_ref, with_cos_ref, with_sin_ref, slots, kernel_sems, ahead_sem, gathered, *rest = rest
        map_ref, sems, *work = rest
        own = lax.axis_index("snap")
        map_copy = pltpu.make_async_copy(map_hbm, map_ref, sems.at[0])
        map_copy.start()
        weights = kernel_copies(kernel_ref, slots, kernel_sems, [own], local_snaps, range(groups))
        for copy in weights[: slots.shape[0]]:
            copy.start()
        ahead = ahead_copy(kernel_ref, ahead_ref, ahead_sem, 0, snap_count)
        ahead.start()
        fence(cube_ref)
        m_ref[TABLE_ROWS:, :] = jnp.zeros((LANES - TABLE_ROWS, pixels), jnp.bfloat16)
        for b in range(blocks):
            part = slice(b * width, (b + 1) * width)
            l_ref[:, part] = table(lm_ref[0:1, part])
            m_ref[:TABLE_ROWS, part] = table(lm_ref[1:2, part]).astype(jnp.bfloat16)
        pick_v(uv_ref, columns_ref, with_cos_ref, with_sin_ref, cells)
        map_copy.wait()
        collect(lambda s: None, own, [own], map_ref, buffer, beam_ref, work[:2], work[2:], [[gathered]])
        rows = GROUP * chans
        for g in range(groups):
            n = g % slots.shape[0]
            weights[g].wait()
            group_tiles = gathered[g * rows : (g + 1) * rows, :]
            for i in range(GROUP):
                start = g * rows + i * chans
                cube_ref[start : start + chans, :] = group_term(group_tiles, slots.at[n], i, chans)
            if g + slots.shape[0] < groups:
                weights[g + slots.shape[0]].start()
        ahead.wait()

    return pl.pallas_call(
        body,
        out_shape=(
            pltpu.VMEM((blocks * chans, width), jnp.float32),
            pltpu.VMEM((TABLE_ROWS, pixels), jnp.float32),
            pltpu.VMEM((LANES, pixels), jnp.bfloat16),
            pltpu.VMEM((local_snaps, GROUP, pix, width), jnp.bfloat16),
            pltpu.VMEM((2, columns), jnp.int32),
            pltpu.VMEM((LANES, columns), jnp.bfloat16),
            pltpu.VMEM((LANES, columns), jnp.bfloat16),
        ),
        in_specs=[HBM, VMEM, VMEM, HBM, VMEM, VMEM],
        out_specs=(VMEM,) * 7,
        scratch_shapes=[
            *kernel_scratch(kernel, local_snaps, groups),
            pltpu.SemaphoreType.DMA,
            pltpu.VMEM((blocks * chans, local_snaps * pix), jnp.bfloat16),
            *tile_scratch(tile_map, snap_tiles, blocks, 1),
        ],
        compiler_params=limit(24),
        name="own_part",
    )(tile_map, snap_tiles, beam_gain, kernel, pixel_lm, mode_uv)


def pick_v(uv_ref, columns_ref, with_cos_ref, with_sin_ref, cells):
    chunk = 2 * LANES
    lane = lax.broadcasted_iota(jnp.int32, (1, chunk), 1)
    row = lax.broadcasted_iota(jnp.int32, (TABLE_ROWS, chunk), 0)
    for start in range(0, columns_ref.shape[1], chunk):
        part = slice(start, start + chunk)
        is_imag = lax.rem(lane, 2 * cells) >= cells
        modes = uv_ref[:, start // 2 : start // 2 + LANES]
        owned = [modes[:, k : k + cells] for k in range(0, LANES, cells)]
        both = jnp.concatenate([piece for piece in owned for _ in range(2)], axis=1)
        columns_ref[:, part] = both
        u, v = both[0:1], both[1:2]
        sign_u = jnp.where(u < 0, -1.0, 1.0)
        sign_v = jnp.where(v < 0, -1.0, 1.0)
        v = jnp.abs(v)
        sin_row = jnp.where(v == 0, -1, SINE_ROW + lax.rem(v, UV_MAX))
        with_cos = jnp.where(row == jnp.where(is_imag, sin_row, v), jnp.where(is_imag, -sign_v, 1.0), 0.0)
        with_sin = jnp.where(
            row == jnp.where(is_imag, v, sin_row), jnp.where(is_imag, -sign_u, -sign_u * sign_v), 0.0
        )
        empty = jnp.zeros((LANES - TABLE_ROWS, chunk), jnp.float32)
        with_cos_ref[:, part] = jnp.concatenate([with_cos, empty]).astype(jnp.bfloat16)
        with_sin_ref[:, part] = jnp.concatenate([with_sin, empty]).astype(jnp.bfloat16)


def uv_part(others, kernel, ahead, partial, l_table, m_table, first_group, chans, begun=None, picks=None, cells=0):
    snap_count = len(others) + 1
    _, blocks, pix, width = kernel.shape
    local_snaps = others[0].shape[1] // pix
    rows = GROUP * chans
    groups = range(first_group, first_group + others[0].shape[0] // rows)
    high, q = padded(chans), together(chans)
    span, tail = UV_MAX * chans, q * chans
    grid_rows = 2 * span + tail
    later = len(others) - 1
    last = begun is not None

    def select(lhs, columns_ref, with_cos_ref, with_sin_ref, out_ref):
        chunk = 2 * LANES
        which = lax.broadcasted_iota(jnp.int32, (tail, chunk), 0) // chans
        for start in range(0, columns_ref.shape[1], chunk):
            part = slice(start, start + chunk)
            picks = jnp.concatenate([with_cos_ref[:, part], with_sin_ref[:, part]])
            at_v = jnp.dot(lhs[...], picks, preferred_element_type=jnp.float32)
            first_u = jnp.abs(columns_ref[0:1, part]) - which
            picked = jnp.zeros((tail, chunk), jnp.float32)
            for k in range(0, UV_MAX + 1, q):
                picked = jnp.where(first_u == k, at_v[k * chans : k * chans + tail], picked)
            value = picked[:chans]
            for k in range(1, q):
                value += picked[k * chans : (k + 1) * chans]
            if high > chans:
                value = jnp.concatenate([value, jnp.zeros((high - chans, chunk), jnp.float32)])
            value = value.astype(jnp.bfloat16)
            for k in range(0, chunk, 2 * cells):
                out_ref[(start + k) // (2 * cells)] = value[:, k : k + 2 * cells]

    def body(*rest):
        tiles_refs, rest = rest[: len(others)], rest[len(others) :]
        kernel_ref, ahead_ref, partial_ref, l_ref, m_ref, *rest = rest
        if last:
            begun_cube, begun_acc, columns_ref, with_cos_ref, with_sin_ref, sky_ref, out_ref, acc, lhs, *rest = rest
        else:
            cube_ref, acc, next_ref, fetched, fetch_sems, *rest = rest
            following = [
                ahead_copy(kernel_ref, fetched, fetch_sems.at[0], GROUP, snap_count),
                ahead_copy(kernel_ref, next_ref, fetch_sems.at[1], groups.stop * GROUP, snap_count),
            ]
            for copy in following:
                copy.start()
            fence(acc)
        if later:
            slots, sems = rest
            own = lax.axis_index("snap")
            sources = [lax.rem(own + snap_count - j, snap_count) for j in range(2, snap_count)]
            weights = kernel_copies(kernel_ref, slots, sems, sources, local_snaps, groups)
            for copy in weights[: slots.shape[0]]:
                copy.start()
        which = lax.broadcasted_iota(jnp.int32, (tail, width), 0) // chans
        if last:
            for b in range(first_group * GROUP):
                sky_ref[:, b, :] = begun_cube[b * chans : (b + 1) * chans, :]
        for n, g in enumerate(groups):
            sky = [partial_ref[g * rows + i * chans : g * rows + (i + 1) * chans, :] for i in range(GROUP)]
            near, at = ahead_ref, n * GROUP
            if not last and n > 0:
                near, at = fetched, at - GROUP
                if n == 1:
                    following[0].wait()
            near = near.at[:, at : at + GROUP]
            group_tiles = tiles_refs[0][n * rows : (n + 1) * rows, :]
            sky = [sky[i] + group_term(group_tiles, near, i, chans) for i in range(GROUP)]
            for j in range(later):
                item = n * later + j
                weights[item].wait()
                group_tiles = tiles_refs[j + 1][n * rows : (n + 1) * rows, :]
                slot = slots.at[item % slots.shape[0]]
                sky = [sky[i] + group_term(group_tiles, slot, i, chans) for i in range(GROUP)]
                if item + slots.shape[0] < len(weights):
                    weights[item + slots.shape[0]].start()
            for i in range(GROUP):
                b = g * GROUP + i
                part = slice(b * width, (b + 1) * width)
                if last:
                    sky_ref[:, b, :] = sky[i]
                else:
                    cube_ref[b * chans : (b + 1) * chans, :] = sky[i]
                low = sky[i].astype(jnp.bfloat16).astype(jnp.float32)
                low = jnp.concatenate([low] * q)
                waves = []
                for r in [*range(0, UV_MAX, q), *range(SINE_ROW, TABLE_ROWS, q), UV_MAX]:
                    wave = l_ref[r : r + 1, part]
                    for k in range(1, q):
                        wave = jnp.where(which < k, wave, l_ref[r + k : r + k + 1, part])
                    waves.append(wave * low)
                waves = jnp.concatenate(waves).astype(jnp.bfloat16)
                term = lax.dot_general(
                    waves, m_ref[:, part], (((1,), (1,)), ((), ())), preferred_element_type=jnp.float32
                )
                if n or i:
                    acc[...] += term
                elif last:
                    acc[...] = begun_acc[...] + term
                else:
                    acc[...] = term
        if last:
            row = lax.broadcasted_iota(jnp.int32, (span, LANES), 0)
            sines = acc[span : 2 * span, :]
            lhs[:span, :LANES] = acc[:span, :].astype(jnp.bfloat16)
            lhs[span:, :LANES] = acc[2 * span :, :].astype(jnp.bfloat16)
            lhs[:span, LANES:] = jnp.where(row < chans, 0.0, sines).astype(jnp.bfloat16)
            lhs[span:, LANES:] = jnp.where(row[:tail] < chans, sines[:tail], 0.0).astype(jnp.bfloat16)
            select(lhs, columns_ref, with_cos_ref, with_sin_ref, out_ref)
        else:
            following[1].wait()

    grid_shape = (grid_rows, LANES)
    scratch = []
    operands = [*others, kernel, ahead, partial, l_table, m_table]
    if last:
        columns, with_cos, with_sin = picks
        operands += [*begun, columns, with_cos, with_sin]
        out_shape = (
            pltpu.VMEM((chans, blocks, width), jnp.float32),
            pltpu.VMEM((columns.shape[1] // (2 * cells), high, 2 * cells), jnp.bfloat16),
        )
        scratch += [pltpu.VMEM(grid_shape, jnp.float32), pltpu.VMEM((span + tail, 2 * LANES), jnp.bfloat16)]
    else:
        out_shape = (
            pltpu.VMEM((groups.stop * rows, width), jnp.float32),
            pltpu.VMEM(grid_shape, jnp.float32),
            pltpu.VMEM((local_snaps, blocks - groups.stop * GROUP, pix, width), jnp.bfloat16),
        )
        fetched = (local_snaps, groups.stop * GROUP - GROUP, pix, width)
        scratch += [pltpu.VMEM(fetched, jnp.bfloat16), pltpu.SemaphoreType.DMA((2,))]
    if later:
        scratch += kernel_scratch(kernel, local_snaps, len(groups) * later)
    return pl.pallas_call(
        body,
        out_shape=out_shape,
        in_specs=[HBM if operand is kernel else VMEM for operand in operands],
        out_specs=(VMEM,) * len(out_shape),
        scratch_shapes=scratch,
        compiler_params=limit(24 if later else 12),
        name="uv_last" if last else "uv_first",
    )(*operands)


def delay_part(modes, matrix, cells):
    length = matrix.shape[2] // 4

    def body(modes_ref, matrix_ref, out_ref):
        value = modes_ref[...]
        total = jnp.zeros((cells, 2 * length), jnp.float32)
        for part in range(2):
            columns = value[:, part * cells : (part + 1) * cells]
            for piece in range(2):
                total += lax.dot_general(
                    columns,
                    matrix_ref[piece, :, part * 2 * length : (part + 1) * 2 * length],
                    (((0,), (0,)), ((), ())),
                    preferred_element_type=jnp.float32,
                )
        for part in range(2):
            out_ref[part] = total[:, part * length : (part + 1) * length]

    return pl.pallas_call(
        body,
        out_shape=jax.ShapeDtypeStruct((2, cells, length), jnp.float32),
        in_specs=[VMEM, VMEM],
        out_specs=VMEM,
        compiler_params=limit(8),
        name="delay_part",
    )(modes, matrix)


def per_device(snap_tiles, beam_gain, kernel, tile_map, pixel_lm, mode_uv):
    snap_count = lax.axis_size("snap")
    chan_count = lax.axis_size("chan")
    chans = snap_tiles.shape[1]
    high = padded(chans)
    length = chans * chan_count
    owners = snap_count * chan_count
    cells = mode_uv.shape[1] // owners
    pixel_total = pixel_lm.shape[1] * snap_count

    snap_tiles, beam_gain, kernel, tile_map, pixel_lm, mode_uv = (
        pltpu.with_memory_space_constraint(value, pltpu.HBM)
        for value in (snap_tiles, beam_gain, kernel, tile_map, pixel_lm, mode_uv)
    )
    *sent, snap_tiles, beam_gain, pixel_lm, mode_uv = gather_tiles(
        tile_map, snap_tiles, beam_gain, pixel_lm, mode_uv, snap_count
    )
    others = [
        lax.ppermute(part, "snap", [(i, (i + n // PARTS + 1) % snap_count) for i in range(snap_count)])
        for n, part in enumerate(sent)
    ]
    partial, l_table, m_table, ahead, *picks = own_part(
        tile_map, snap_tiles, beam_gain, kernel, pixel_lm, mode_uv, cells, snap_count
    )
    shared = (partial, l_table, m_table)
    *begun, ahead_next = uv_part(others[0::PARTS], kernel, ahead, *shared, 0, chans)
    half = kernel.shape[1] // GROUP // PARTS
    sky, spread = uv_part(others[1::PARTS], kernel, ahead_next, *shared, half, chans, begun, picks, cells)
    regrouped = lax.all_to_all(spread, ("snap", "chan"), 0, 0, tiled=True)
    matrix = delay_matrix(length) / math.sqrt(pixel_total)
    matrix = matrix.transpose(1, 0, 2, 3).reshape(chan_count, chans, 4 * length)
    matrix = np.pad(matrix, ((0, 0), (0, high - chans), (0, 0))).reshape(chan_count * high, 4 * length)
    matrix = np.concatenate([matrix] * snap_count)
    upper = matrix.astype(jnp.bfloat16)
    lower = (matrix - upper.astype(np.float64)).astype(jnp.bfloat16)
    delay = delay_part(
        regrouped.reshape(owners * high, 2 * cells), jnp.asarray(np.stack([upper, lower])), cells
    )
    return (sky.transpose(1, 0, 2), delay.transpose(0, 2, 1))


def solution(mesh):
    return jax.shard_map(
        per_device,
        mesh=mesh,
        in_specs=(
            P("snap", "chan", None, None),
            P("snap", None, None),
            P(None, "snap", None, None),
            P(),
            P(None, "snap"),
            P(),
        ),
        out_specs=(P("snap", "chan", None), P(None, None, ("snap", "chan"))),
        check_vma=False,
    )
```

```python
import math

import jax
import jax.numpy as jnp
import numpy as np
from jax import lax
from jax.experimental import pallas as pl
from jax.experimental.pallas import tpu as pltpu
from jax.sharding import PartitionSpec as P

LANES = 128
SUBLANES = 8
GROUP = 4
PARTS = 2
UV_MAX = 32
SINE_ROW = 40
TABLE_ROWS = SINE_ROW + UV_MAX

VMEM = pl.BlockSpec(memory_space=pltpu.VMEM)
HBM = pl.BlockSpec(memory_space=pltpu.HBM)


def limit(mebibytes):
    return pltpu.CompilerParams(vmem_limit_bytes=mebibytes << 20)


def padded(chans):
    return -(-chans // SUBLANES) * SUBLANES


def together(chans):
    return SUBLANES // math.gcd(SUBLANES, chans)


def delay_matrix(length):
    index = np.arange(length)
    window = 0.54 - 0.46 * np.cos(index * (2.0 * math.pi / (length - 1)))
    phase = (index[:, None] * index[None, :] % length) * (2.0 * math.pi / length)
    scale = window[:, None] / math.sqrt(length)
    cosine, sine = np.cos(phase) * scale, np.sin(phase) * scale
    return np.stack([np.stack([cosine, -sine], 1), np.stack([sine, cosine], 1)])


def cos_turns(angle):
    r = angle - jnp.round(angle)
    square = r * r
    series = jnp.float32(0.0)
    for power in (11, 9, 7, 5, 3, 1):
        term = math.pi**power / math.factorial(power) * (-1.0) ** (power // 2)
        series = series * square + term
    sine = series * r
    return 1.0 - 2.0 * sine * sine


def table(coord):
    shape = (SUBLANES, coord.shape[1])
    row = lax.broadcasted_iota(jnp.int32, shape, 0)
    steps = UV_MAX // SUBLANES
    fine = row.astype(jnp.float32) * coord
    fine_cos, fine_sin = cos_turns(fine), cos_turns(fine - 0.25)
    coarse_k = ((lax.rem(row, steps) + 1) * SUBLANES).astype(jnp.float32)
    coarse = cos_turns(coarse_k * coord - jnp.where(row < steps, 0.0, 0.25))
    cosines, sines = [fine_cos], [fine_sin]
    for a in range(1, steps + 1):
        step_cos, step_sin = coarse[a - 1 : a], coarse[steps + a - 1 : steps + a]
        cosines.append(step_cos * fine_cos - step_sin * fine_sin)
        sines.append(step_sin * fine_cos + step_cos * fine_sin)
    cosines[-1] = jnp.where(row > 0, 0.0, cosines[-1])
    sines[0] = jnp.where(row > 0, sines[0], sines.pop())
    return jnp.concatenate([*cosines, *sines])


def tile_scratch(tile_map, snap_tiles, blocks, copies):
    local_snaps, chans, tiles, pix = snap_tiles.shape
    pitch = tiles + SUBLANES
    return [
        pltpu.SMEM(tile_map.shape, jnp.int32),
        pltpu.SemaphoreType.DMA((copies,)),
        *[pltpu.VMEM((padded(chans) * pitch, pix), jnp.float32)] * 2,
        *[pltpu.VMEM((blocks * chans, pix), jnp.float32)] * 2,
    ]


def collect(ready, own, dests, map_ref, buffer, beam_ref, spread, stage, outs):
    local_snaps, chans, tiles, pix = buffer.shape
    blocks = stage[0].shape[0] // chans
    pitch = tiles + SUBLANES
    for s in range(local_snaps):
        ready(s)
        wide = spread[s % 2]
        for c in range(chans):
            wide[c * pitch : c * pitch + tiles, :] = buffer[s, c].astype(jnp.float32) * beam_ref[s]
        for n, (dest, parts) in enumerate(zip(dests, outs)):
            rows = stage[(s + n) % 2]
            for b in range(blocks):
                t = map_ref[own * local_snaps + s, dest * blocks + b]
                rows[b * chans : (b + 1) * chans, :] = wide[pl.ds(t, chans, stride=pitch), :]
            for i, out in enumerate(parts):
                size = out.shape[0]
                out[:, s * pix : (s + 1) * pix] = rows[i * size : (i + 1) * size, :].astype(jnp.bfloat16)


def gather_tiles(tile_map, snap_tiles, beam_gain, pixel_lm, mode_uv, snap_count):
    local_snaps, chans, tiles, pix = snap_tiles.shape
    blocks = tile_map.shape[1] // snap_count
    count = (snap_count - 1) * PARTS
    fetched = (snap_tiles, beam_gain, pixel_lm, mode_uv)

    def body(map_hbm, tiles_hbm, beam_hbm, lm_hbm, uv_hbm, *rest):
        outs, (buffer, beam_ref, lm_ref, uv_ref, map_ref, sems, *work) = rest[:count], rest[count:]
        copies = [
            pltpu.make_async_copy(source, target, sems.at[local_snaps + n])
            for n, (source, target) in enumerate(
                [(map_hbm, map_ref), (beam_hbm, beam_ref), (lm_hbm, lm_ref), (uv_hbm, uv_ref)]
            )
        ]
        of_snap = [
            pltpu.make_async_copy(tiles_hbm.at[s], buffer.at[s], sems.at[s]) for s in range(local_snaps)
        ]
        for copy in [*copies[:2], *of_snap, *copies[2:]]:
            copy.start()
        own = lax.axis_index("snap")
        dests = [lax.rem(own + j, snap_count) for j in range(1, snap_count)]
        outs = [outs[n : n + PARTS] for n in range(0, count, PARTS)]

        def ready(s):
            if s == 0:
                copies[0].wait()
                copies[1].wait()
            of_snap[s].wait()

        collect(ready, own, dests, map_ref, buffer, beam_ref, work[:2], work[2:], outs)
        copies[2].wait()
        copies[3].wait()

    return pl.pallas_call(
        body,
        out_shape=[
            *[pltpu.VMEM((blocks // PARTS * chans, local_snaps * pix), jnp.bfloat16)] * count,
            *[pltpu.VMEM(value.shape, value.dtype) for value in fetched],
        ],
        in_specs=[HBM] * 5,
        out_specs=[VMEM] * (count + len(fetched)),
        scratch_shapes=tile_scratch(tile_map, snap_tiles, blocks, local_snaps + 4),
        compiler_params=limit(8),
        name="gather_tiles",
    )(tile_map, *fetched)


def kernel_copies(kernel_ref, slots, sems, sources, local_snaps, groups):
    copies = []
    for g in groups:
        for source in sources:
            n = len(copies) % slots.shape[0]
            copies.append(
                pltpu.make_async_copy(
                    kernel_ref.at[pl.ds(source * local_snaps, local_snaps), pl.ds(g * GROUP, GROUP)],
                    slots.at[n],
                    sems.at[n],
                )
            )
    return copies


def fence(ref):
    @pl.when(lax.axis_index("snap") < 0)
    def _():
        ref[...] = jnp.zeros(ref.shape, ref.dtype)


def ahead_copy(kernel_ref, ahead_ref, sem, first_block, snap_count):
    local_snaps, blocks = ahead_ref.shape[:2]
    source = lax.rem(lax.axis_index("snap") + snap_count - 1, snap_count)
    return pltpu.make_async_copy(
        kernel_ref.at[pl.ds(source * local_snaps, local_snaps), pl.ds(first_block, blocks)], ahead_ref, sem
    )


def kernel_scratch(kernel, local_snaps, items):
    _, _, pix, width = kernel.shape
    slots = min(items, 4)
    return [
        pltpu.VMEM((slots, local_snaps, GROUP, pix, width), jnp.bfloat16),
        pltpu.SemaphoreType.DMA((slots,)),
    ]


def group_term(tiles, slot, i, chans):
    local_snaps, _, pix, width = slot.shape
    weights = slot[:, i].reshape(local_snaps * pix, width)
    term = jnp.dot(tiles, weights, preferred_element_type=jnp.float32)
    return term[i * chans : (i + 1) * chans]


def own_part(tile_map, snap_tiles, beam_gain, kernel, pixel_lm, mode_uv, cells, snap_count):
    local_snaps, chans, tiles, pix = snap_tiles.shape
    blocks, width = kernel.shape[1], kernel.shape[3]
    groups = blocks // GROUP
    pixels = blocks * width
    columns = 2 * mode_uv.shape[1]

    def body(map_hbm, buffer, beam_ref, kernel_ref, lm_ref, uv_ref, cube_ref, l_ref, m_ref, *rest):
        ahead_ref, columns_ref, with_cos_ref, with_sin_ref, slots, kernel_sems, ahead_sem, gathered, *rest = rest
        map_ref, sems, *work = rest
        own = lax.axis_index("snap")
        map_copy = pltpu.make_async_copy(map_hbm, map_ref, sems.at[0])
        map_copy.start()
        weights = kernel_copies(kernel_ref, slots, kernel_sems, [own], local_snaps, range(groups))
        for copy in weights[: slots.shape[0]]:
            copy.start()
        ahead = ahead_copy(kernel_ref, ahead_ref, ahead_sem, 0, snap_count)
        ahead.start()
        fence(cube_ref)
        m_ref[TABLE_ROWS:, :] = jnp.zeros((LANES - TABLE_ROWS, pixels), jnp.bfloat16)
        for b in range(blocks):
            part = slice(b * width, (b + 1) * width)
            l_ref[:, part] = table(lm_ref[0:1, part])
            m_ref[:TABLE_ROWS, part] = table(lm_ref[1:2, part]).astype(jnp.bfloat16)
        pick_v(uv_ref, columns_ref, with_cos_ref, with_sin_ref, cells)
        map_copy.wait()
        collect(lambda s: None, own, [own], map_ref, buffer, beam_ref, work[:2], work[2:], [[gathered]])
        rows = GROUP * chans
        for g in range(groups):
            n = g % slots.shape[0]
            weights[g].wait()
            group_tiles = gathered[g * rows : (g + 1) * rows, :]
            for i in range(GROUP):
                start = g * rows + i * chans
                cube_ref[start : start + chans, :] = group_term(group_tiles, slots.at[n], i, chans)
            if g + slots.shape[0] < groups:
                weights[g + slots.shape[0]].start()
        ahead.wait()

    return pl.pallas_call(
        body,
        out_shape=(
            pltpu.VMEM((blocks * chans, width), jnp.float32),
            pltpu.VMEM((TABLE_ROWS, pixels), jnp.float32),
            pltpu.VMEM((LANES, pixels), jnp.bfloat16),
            pltpu.VMEM((local_snaps, GROUP, pix, width), jnp.bfloat16),
            pltpu.VMEM((2, columns), jnp.int32),
            pltpu.VMEM((LANES, columns), jnp.bfloat16),
            pltpu.VMEM((LANES, columns), jnp.bfloat16),
        ),
        in_specs=[HBM, VMEM, VMEM, HBM, VMEM, VMEM],
        out_specs=(VMEM,) * 7,
        scratch_shapes=[
            *kernel_scratch(kernel, local_snaps, groups),
            pltpu.SemaphoreType.DMA,
            pltpu.VMEM((blocks * chans, local_snaps * pix), jnp.bfloat16),
            *tile_scratch(tile_map, snap_tiles, blocks, 1),
        ],
        compiler_params=limit(24),
        name="own_part",
    )(tile_map, snap_tiles, beam_gain, kernel, pixel_lm, mode_uv)


def pick_v(uv_ref, columns_ref, with_cos_ref, with_sin_ref, cells):
    chunk = 2 * LANES
    lane = lax.broadcasted_iota(jnp.int32, (1, chunk), 1)
    row = lax.broadcasted_iota(jnp.int32, (TABLE_ROWS, chunk), 0)
    for start in range(0, columns_ref.shape[1], chunk):
        part = slice(start, start + chunk)
        is_imag = lax.rem(lane, 2 * cells) >= cells
        modes = uv_ref[:, start // 2 : start // 2 + LANES]
        owned = [modes[:, k : k + cells] for k in range(0, LANES, cells)]
        both = jnp.concatenate([piece for piece in owned for _ in range(2)], axis=1)
        columns_ref[:, part] = both
        u, v = both[0:1], both[1:2]
        sign_u = jnp.where(u < 0, -1.0, 1.0)
        sign_v = jnp.where(v < 0, -1.0, 1.0)
        v = jnp.abs(v)
        sin_row = jnp.where(v == 0, -1, SINE_ROW + lax.rem(v, UV_MAX))
        with_cos = jnp.where(row == jnp.where(is_imag, sin_row, v), jnp.where(is_imag, -sign_v, 1.0), 0.0)
        with_sin = jnp.where(
            row == jnp.where(is_imag, v, sin_row), jnp.where(is_imag, -sign_u, -sign_u * sign_v), 0.0
        )
        empty = jnp.zeros((LANES - TABLE_ROWS, chunk), jnp.float32)
        with_cos_ref[:, part] = jnp.concatenate([with_cos, empty]).astype(jnp.bfloat16)
        with_sin_ref[:, part] = jnp.concatenate([with_sin, empty]).astype(jnp.bfloat16)


def uv_part(others, kernel, ahead, partial, l_table, m_table, first_group, chans, begun=None, picks=None, cells=0):
    snap_count = len(others) + 1
    _, blocks, pix, width = kernel.shape
    local_snaps = others[0].shape[1] // pix
    rows = GROUP * chans
    groups = range(first_group, first_group + others[0].shape[0] // rows)
    high, q = padded(chans), together(chans)
    span, tail = UV_MAX * chans, q * chans
    grid_rows = 2 * span + tail
    later = len(others) - 1
    last = begun is not None

    def select(lhs, columns_ref, with_cos_ref, with_sin_ref, out_ref):
        chunk = 2 * LANES
        which = lax.broadcasted_iota(jnp.int32, (tail, chunk), 0) // chans
        for start in range(0, columns_ref.shape[1], chunk):
            part = slice(start, start + chunk)
            picks = jnp.concatenate([with_cos_ref[:, part], with_sin_ref[:, part]])
            at_v = jnp.dot(lhs[...], picks, preferred_element_type=jnp.float32)
            first_u = jnp.abs(columns_ref[0:1, part]) - which
            picked = jnp.zeros((tail, chunk), jnp.float32)
            for k in range(0, UV_MAX + 1, q):
                picked = jnp.where(first_u == k, at_v[k * chans : k * chans + tail], picked)
            value = picked[:chans]
            for k in range(1, q):
                value += picked[k * chans : (k + 1) * chans]
            if high > chans:
                value = jnp.concatenate([value, jnp.zeros((high - chans, chunk), jnp.float32)])
            value = value.astype(jnp.bfloat16)
            for k in range(0, chunk, 2 * cells):
                out_ref[(start + k) // (2 * cells)] = value[:, k : k + 2 * cells]

    def body(*rest):
        tiles_refs, rest = rest[: len(others)], rest[len(others) :]
        kernel_ref, ahead_ref, partial_ref, l_ref, m_ref, *rest = rest
        if last:
            begun_cube, begun_acc, columns_ref, with_cos_ref, with_sin_ref, sky_ref, out_ref, acc, lhs, *rest = rest
        else:
            cube_ref, acc, next_ref, fetched, fetch_sems, *rest = rest
            following = [
                ahead_copy(kernel_ref, fetched, fetch_sems.at[0], GROUP, snap_count),
                ahead_copy(kernel_ref, next_ref, fetch_sems.at[1], groups.stop * GROUP, snap_count),
            ]
            for copy in following:
                copy.start()
            fence(acc)
        if later:
            slots, sems = rest
            own = lax.axis_index("snap")
            sources = [lax.rem(own + snap_count - j, snap_count) for j in range(2, snap_count)]
            weights = kernel_copies(kernel_ref, slots, sems, sources, local_snaps, groups)
            for copy in weights[: slots.shape[0]]:
                copy.start()
        which = lax.broadcasted_iota(jnp.int32, (tail, width), 0) // chans
        if last:
            for b in range(first_group * GROUP):
                sky_ref[:, b, :] = begun_cube[b * chans : (b + 1) * chans, :]
        for n, g in enumerate(groups):
            sky = [partial_ref[g * rows + i * chans : g * rows + (i + 1) * chans, :] for i in range(GROUP)]
            near, at = ahead_ref, n * GROUP
            if not last and n > 0:
                near, at = fetched, at - GROUP
                if n == 1:
                    following[0].wait()
            near = near.at[:, at : at + GROUP]
            group_tiles = tiles_refs[0][n * rows : (n + 1) * rows, :]
            sky = [sky[i] + group_term(group_tiles, near, i, chans) for i in range(GROUP)]
            for j in range(later):
                item = n * later + j
                weights[item].wait()
                group_tiles = tiles_refs[j + 1][n * rows : (n + 1) * rows, :]
                slot = slots.at[item % slots.shape[0]]
                sky = [sky[i] + group_term(group_tiles, slot, i, chans) for i in range(GROUP)]
                if item + slots.shape[0] < len(weights):
                    weights[item + slots.shape[0]].start()
            for i in range(GROUP):
                b = g * GROUP + i
                part = slice(b * width, (b + 1) * width)
                if last:
                    sky_ref[:, b, :] = sky[i]
                else:
                    cube_ref[b * chans : (b + 1) * chans, :] = sky[i]
                low = sky[i].astype(jnp.bfloat16).astype(jnp.float32)
                low = jnp.concatenate([low] * q)
                waves = []
                for r in [*range(0, UV_MAX, q), *range(SINE_ROW, TABLE_ROWS, q), UV_MAX]:
                    wave = l_ref[r : r + 1, part]
                    for k in range(1, q):
                        wave = jnp.where(which < k, wave, l_ref[r + k : r + k + 1, part])
                    waves.append(wave * low)
                waves = jnp.concatenate(waves).astype(jnp.bfloat16)
                term = lax.dot_general(
                    waves, m_ref[:, part], (((1,), (1,)), ((), ())), preferred_element_type=jnp.float32
                )
                if n or i:
                    acc[...] += term
                elif last:
                    acc[...] = begun_acc[...] + term
                else:
                    acc[...] = term
        if last:
            row = lax.broadcasted_iota(jnp.int32, (span, LANES), 0)
            sines = acc[span : 2 * span, :]
            lhs[:span, :LANES] = acc[:span, :].astype(jnp.bfloat16)
            lhs[span:, :LANES] = acc[2 * span :, :].astype(jnp.bfloat16)
            lhs[:span, LANES:] = jnp.where(row < chans, 0.0, sines).astype(jnp.bfloat16)
            lhs[span:, LANES:] = jnp.where(row[:tail] < chans, sines[:tail], 0.0).astype(jnp.bfloat16)
            select(lhs, columns_ref, with_cos_ref, with_sin_ref, out_ref)
        else:
            following[1].wait()

    grid_shape = (grid_rows, LANES)
    scratch = []
    operands = [*others, kernel, ahead, partial, l_table, m_table]
    if last:
        columns, with_cos, with_sin = picks
        operands += [*begun, columns, with_cos, with_sin]
        out_shape = (
            pltpu.VMEM((chans, blocks, width), jnp.float32),
            pltpu.VMEM((columns.shape[1] // (2 * cells), high, 2 * cells), jnp.bfloat16),
        )
        scratch += [pltpu.VMEM(grid_shape, jnp.float32), pltpu.VMEM((span + tail, 2 * LANES), jnp.bfloat16)]
    else:
        out_shape = (
            pltpu.VMEM((groups.stop * rows, width), jnp.float32),
            pltpu.VMEM(grid_shape, jnp.float32),
            pltpu.VMEM((local_snaps, blocks - groups.stop * GROUP, pix, width), jnp.bfloat16),
        )
        fetched = (local_snaps, groups.stop * GROUP - GROUP, pix, width)
        scratch += [pltpu.VMEM(fetched, jnp.bfloat16), pltpu.SemaphoreType.DMA((2,))]
    if later:
        scratch += kernel_scratch(kernel, local_snaps, len(groups) * later)
    return pl.pallas_call(
        body,
        out_shape=out_shape,
        in_specs=[HBM if operand is kernel else VMEM for operand in operands],
        out_specs=(VMEM,) * len(out_shape),
        scratch_shapes=scratch,
        compiler_params=limit(24 if later else 12),
        name="uv_last" if last else "uv_first",
    )(*operands)


def delay_part(modes, matrix, cells):
    length = matrix.shape[2] // 4

    def body(modes_ref, matrix_ref, out_ref):
        value = modes_ref[...]
        total = jnp.zeros((cells, 2 * length), jnp.float32)
        for part in range(2):
            columns = value[:, part * cells : (part + 1) * cells]
            for piece in range(2):
                total += lax.dot_general(
                    columns,
                    matrix_ref[piece, :, part * 2 * length : (part + 1) * 2 * length],
                    (((0,), (0,)), ((), ())),
                    preferred_element_type=jnp.float32,
                )
        for part in range(2):
            out_ref[part] = total[:, part * length : (part + 1) * length]

    return pl.pallas_call(
        body,
        out_shape=jax.ShapeDtypeStruct((2, cells, length), jnp.float32),
        in_specs=[VMEM, VMEM],
        out_specs=VMEM,
        compiler_params=limit(8),
        name="delay_part",
    )(modes, matrix)


def per_device(snap_tiles, beam_gain, kernel, tile_map, pixel_lm, mode_uv):
    snap_count = lax.axis_size("snap")
    chan_count = lax.axis_size("chan")
    chans = snap_tiles.shape[1]
    high = padded(chans)
    length = chans * chan_count
    owners = snap_count * chan_count
    cells = mode_uv.shape[1] // owners
    pixel_total = pixel_lm.shape[1] * snap_count

    snap_tiles, beam_gain, kernel, tile_map, pixel_lm, mode_uv = (
        pltpu.with_memory_space_constraint(value, pltpu.HBM)
        for value in (snap_tiles, beam_gain, kernel, tile_map, pixel_lm, mode_uv)
    )
    *sent, snap_tiles, beam_gain, pixel_lm, mode_uv = gather_tiles(
        tile_map, snap_tiles, beam_gain, pixel_lm, mode_uv, snap_count
    )
    others = [
        lax.ppermute(part, "snap", [(i, (i + n // PARTS + 1) % snap_count) for i in range(snap_count)])
        for n, part in enumerate(sent)
    ]
    partial, l_table, m_table, ahead, *picks = own_part(
        tile_map, snap_tiles, beam_gain, kernel, pixel_lm, mode_uv, cells, snap_count
    )
    shared = (partial, l_table, m_table)
    *begun, ahead_next = uv_part(others[0::PARTS], kernel, ahead, *shared, 0, chans)
    half = kernel.shape[1] // GROUP // PARTS
    sky, spread = uv_part(others[1::PARTS], kernel, ahead_next, *shared, half, chans, begun, picks, cells)
    regrouped = lax.all_to_all(spread, ("snap", "chan"), 0, 0, tiled=True)
    matrix = delay_matrix(length) / math.sqrt(pixel_total)
    matrix = matrix.transpose(1, 0, 2, 3).reshape(chan_count, chans, 4 * length)
    matrix = np.pad(matrix, ((0, 0), (0, high - chans), (0, 0))).reshape(chan_count * high, 4 * length)
    matrix = np.concatenate([matrix] * snap_count)
    upper = matrix.astype(jnp.bfloat16)
    lower = (matrix - upper.astype(np.float64)).astype(jnp.bfloat16)
    delay = delay_part(
        regrouped.reshape(owners * high, 2 * cells), jnp.asarray(np.stack([upper, lower])), cells
    )
    return (sky.transpose(1, 0, 2), delay.transpose(0, 2, 1))


def solution(mesh):
    return jax.shard_map(
        per_device,
        mesh=mesh,
        in_specs=(
            P("snap", "chan", None, None),
            P("snap", None, None),
            P(None, "snap", None, None),
            P(),
            P(None, "snap"),
            P(),
        ),
        out_specs=(P("snap", "chan", None), P(None, None, ("snap", "chan"))),
        check_vma=False,
    )
```
